32 devices in a mesh: groups: 2 (over y), seq: 4 (over z), tensor: 2 (over x), sub: 2 (over core).
Axes of the slice: x: 2, y: 2, z: 4, core: 2. Of those that a mesh axis runs over, the one named last changes fastest.
Arguments:
- features: bfloat16 [3072, 3, 8192], P(('groups', 'seq'), None, ('tensor', 'sub')), parts along dimension 0, may hold values from -6 to 6
- short_filter: float32 [7, 8192], P(None, ('tensor', 'sub')), may hold values from -5 to 5
- medium_filter: float32 [128, 8192], P(None, ('tensor', 'sub')), may hold values from -1.25 to 1.25
- skip_gain: float32 [8192], P(('tensor', 'sub')), may hold values from 0.5 to 1.5
- attn_query: bfloat16 [3072, 8192], P(('groups', 'seq'), ('tensor', 'sub')), parts along dimension 0, may hold values from -100 to 100
- attn_key: bfloat16 [3072, 8192], P(('groups', 'seq'), ('tensor', 'sub')), parts along dimension 0, may hold values from -5 to 5
- attn_value: bfloat16 [3072, 8192], P(('groups', 'seq'), ('tensor', 'sub')), parts along dimension 0, may hold values from -6 to 6
- lengths: int32 [8], P('groups'), parts along dimension 0, may hold values from 1 to 768, 1536 in all
Outputs:
- hyena_out: bfloat16 [3072, 8192], P(('groups', 'seq'), ('tensor', 'sub')), parts along dimension 0
- attn_out: bfloat16 [3072, 8192], P(('groups', 'seq'), ('tensor', 'sub')), parts along dimension 0
The draws below stay inside these ranges and needn't reach their ends.
There are 2 independent parts, one for each index of `groups`. The reference program is written for one: setup_inputs(seed, part) draws one part's arguments, and reference() takes and returns one part's arrays. A program takes and returns all parts, laid end to end along the dimension named above; an argument that names none is the same for every part. Nothing has to cross between parts.
Inputs may be any that keep to these rules, and one draw needn't show every extreme that they name: 4 documents packed end to end in order; their lengths sum to 1536 and the longest is exactly 768 tokens.
All inputs are finite; a program needn't handle non-finite values.
Results may differ from the reference program's by a relative error of at most 0.0051.
Values may be sent and summed in bfloat16 or wider, within the bound.
A program may use at most 192 MiB of HBM per device.

```python
import math
import jax
import jax.numpy as jnp
import numpy as np
from jax import lax

D = 8192
HEADS = 64
HD = 128
SHORT = 7
MEDIUM = 128
DOCS = 4
TOKENS = 1536
MOST = 768


def attention_pair(key):
    base_key = jax.random.fold_in(key, 31)
    query_seed, key_seed = jax.random.split(base_key, 2)
    array_shape = (TOKENS, HEADS * HD)
    key_rows = jnp.clip(jax.random.normal(key_seed, array_shape, jnp.float32), -5.0, 5.0)
    query_rows = jnp.clip(jax.random.normal(query_seed, array_shape, jnp.float32), -5.0, 5.0)
    return (query_rows, key_rows)


def draw_attn_query(key, part):
    return attention_pair(key)[0].astype(jnp.bfloat16)


def draw_attn_key(key, part):
    return attention_pair(key)[1].astype(jnp.bfloat16)


def levels(rng, extent, cuts, smallest, top_value):
    loudness = 1.0
    for position, shards_of in cuts:
        heights = jax.random.uniform(jax.random.fold_in(jax.random.fold_in(rng, 6), position), (shards_of,), jnp.float32, smallest / len(cuts), top_value / len(cuts))
        loudness = loudness * jnp.repeat(jnp.exp(heights), extent[position] // shards_of).reshape((-1,) + (1,) * (len(extent) - 1 - position))
    return loudness


def split_up(amount, total, most, slope):
    loads = [(1 << 20) // math.isqrt(rank ** slope) + 1 for rank in range(2, amount + 1)]
    rest, counts = total - most - (amount - 1), [1] * (amount - 1)
    while rest > 0:
        movable = [i for i in range(amount - 1) if counts[i] < most]
        mass, remaining = sum([loads[i] for i in movable]), rest
        for i in movable:
            more = min(most - counts[i], max(1, remaining * loads[i] // mass), rest)
            counts[i] = counts[i] + more
            rest = rest - more
    return np.array([most] + counts)


def uneven_parts(stream_key, amount, total, reach, skew):
    if amount == 2:
        one = jax.random.randint(stream_key, (), max(1, total - reach), min(reach, total - 1) + 1)
        return jnp.stack([one, total - one])
    tallies = jnp.asarray(split_up(amount, total, reach, skew), jnp.int32)
    couples = (amount - 1) // 2
    source_of, receiver = tallies[1:1 + 2 * couples:2], tallies[2:2 + 2 * couples:2]
    margin = jnp.minimum(source_of - 1, reach - receiver)
    passed = jax.random.randint(jax.random.fold_in(stream_key, 1), (couples,), 0, 1 << 20) % (margin + 1)
    tallies = tallies.at[1:1 + 2 * couples:2].set(source_of - passed).at[2:2 + 2 * couples:2].set(receiver + passed)
    return tallies[jax.random.permutation(jax.random.fold_in(stream_key, 2), amount)]


def noise(rng, dims, width, reach, cuts=(), kind=jnp.bfloat16):
    drawn = width * jax.random.normal(rng, dims, jnp.float32)
    if cuts:
        drawn = drawn * levels(rng, dims, cuts, -0.22, 0.18)
    return jnp.clip(drawn, -reach, reach).astype(kind)


def setup_inputs(seed: int = 0, part: int = 0) -> dict:
    seeds = jax.random.split(jax.random.key(seed), 9)
    part_splits = jax.random.split(jax.random.fold_in(seeds[8], part), 9)
    return {
        "features": noise(part_splits[0], (TOKENS, 3, D), 1.0, 6.0, ((0, 4), (2, 4))),
        "short_filter": noise(seeds[1], (SHORT, D), 0.35, 5.0, ((1, 4),), jnp.float32),
        "medium_filter": noise(seeds[2], (MEDIUM, D), 0.09, 1.25, ((1, 4),), jnp.float32),
        "skip_gain": jnp.clip(0.5 + 1.0 * jax.random.uniform(seeds[3], (D,), jnp.float32) ** levels(seeds[3], (D,), ((0, 4),), -0.2, 0.2), 0.5, 1.5),
        "attn_query": draw_attn_query(jax.random.fold_in(jax.random.fold_in(seeds[8], part), 71), part),
        "attn_key": draw_attn_key(jax.random.fold_in(jax.random.fold_in(seeds[8], part), 71), part),
        "attn_value": noise(part_splits[6], (TOKENS, HEADS * HD), 1.0, 6.0, ((0, 4), (1, 4))),
        "lengths": uneven_parts(part_splits[7], DOCS, TOKENS, MOST, 2).astype(jnp.int32),
    }


def doc_of(positions, lengths):
    doc_ends = jnp.cumsum(lengths, dtype=jnp.int32)
    return jnp.sum((positions[:, None] >= doc_ends[None, :]).astype(jnp.int32), axis=1, dtype=jnp.int32)


def reference(features, short_filter, medium_filter, skip_gain, attn_query, attn_key, attn_value, lengths):
    positions = jnp.arange(TOKENS, dtype=jnp.int32)
    docs = doc_of(positions, lengths)
    queries = features[:, 0].astype(jnp.float32)
    gated = (features[:, 1].astype(jnp.float32) * features[:, 2].astype(jnp.float32)).astype(jnp.bfloat16)
    gated = lax.optimization_barrier(gated)
    padded = jnp.concatenate((jnp.zeros((MEDIUM - 1, D), jnp.bfloat16), gated), axis=0)
    pad_docs = jnp.concatenate((jnp.full((MEDIUM - 1,), -1, jnp.int32), docs), axis=0)

    def tap_term(tap_index, filter_bank):
        first_row = (jnp.int32(MEDIUM - 1) - tap_index).astype(jnp.int32)
        window = lax.dynamic_slice_in_dim(padded, first_row, TOKENS, 0).astype(jnp.float32)
        window_docs = lax.dynamic_slice_in_dim(pad_docs, first_row, TOKENS, 0)
        keep_mask = (window_docs == docs).astype(jnp.float32)[:, None]
        taps = lax.dynamic_index_in_dim(filter_bank, tap_index, 0, keepdims=False)
        return taps[None, :] * window * keep_mask

    short_sum = jnp.zeros((TOKENS, D), jnp.float32)
    for tap_index in range(SHORT):
        short_sum = short_sum + tap_term(jnp.int32(tap_index), short_filter)
    medium_sum = lax.fori_loop(0, MEDIUM, lambda tap_index, partial_value: partial_value + tap_term(jnp.asarray(tap_index).astype(jnp.int32), medium_filter), jnp.zeros((TOKENS, D), jnp.float32))
    hyena_out = (queries * (short_sum + medium_sum + skip_gain[None, :] * gated.astype(jnp.float32))).astype(jnp.bfloat16)

    allowed = (positions[None, :] <= positions[:, None]) & (docs[None, :] == docs[:, None])
    score_scale = HD ** -0.5
    query_heads = attn_query.reshape(TOKENS, HEADS, HD).transpose(1, 0, 2)
    key_heads = attn_key.reshape(TOKENS, HEADS, HD).transpose(1, 0, 2)
    value_heads = attn_value.reshape(TOKENS, HEADS, HD).transpose(1, 0, 2)

    def one_head(operands):
        head_q, head_k, head_v = operands
        scores = jnp.dot(head_q, head_k.T, preferred_element_type=jnp.float32) * score_scale
        top_score = jnp.max(jnp.where(allowed, scores, -jnp.inf), axis=1)
        weights = jnp.where(allowed, jnp.exp(scores - top_score[:, None]), 0.0)
        total = jnp.sum(weights, axis=1)
        mixed = jnp.dot(weights.astype(jnp.bfloat16), head_v, preferred_element_type=jnp.float32)
        return (mixed / total[:, None]).astype(jnp.bfloat16)

    head_out = lax.map(one_head, (query_heads, key_heads, value_heads))
    attn_out = head_out.transpose(1, 0, 2).reshape(TOKENS, HEADS * HD)
    return (hyena_out, attn_out)
```

```python
import math

import jax
import jax.numpy as jnp
from jax import lax
from jax.experimental import pallas as pl
from jax.experimental.pallas import tpu as pltpu
from jax.sharding import PartitionSpec as P

HD = 128


def passed_along(value, axis, by):
    length = lax.axis_size(axis)
    pairs = [(i, i + by) for i in range(length) if 0 <= i + by < length]
    return lax.ppermute(value, axis, pairs)


def doc_of(positions, lengths):
    doc_ends = jnp.cumsum(lengths, dtype=jnp.int32)
    return jnp.sum(
        (positions[:, None] >= doc_ends[None, :]).astype(jnp.int32), axis=1, dtype=jnp.int32
    )


def hyena_mix(features, short_filter, medium_filter, skip_gain, lengths):
    row_count = features.shape[0]
    medium_taps = medium_filter.shape[0]
    rim_rows = medium_taps - 1
    span_index = lax.axis_index("seq")
    queries = features[:, 0].astype(jnp.float32)
    gated = (features[:, 1].astype(jnp.float32) * features[:, 2].astype(jnp.float32)).astype(
        jnp.bfloat16
    )
    gated = lax.optimization_barrier(gated)
    carried = passed_along(gated[row_count - rim_rows :], "seq", 1)
    extended = jnp.concatenate((carried, gated), axis=0)
    ext_positions = (
        span_index * row_count - rim_rows + jnp.arange(row_count + rim_rows, dtype=jnp.int32)
    )
    ext_docs = doc_of(ext_positions, lengths)
    ext_live = ext_positions >= 0
    own_docs = ext_docs[rim_rows:]

    def tap_term(tap_index, filter_bank):
        first_row = rim_rows - tap_index
        window = lax.dynamic_slice_in_dim(extended, first_row, row_count, 0).astype(jnp.float32)
        same_doc = lax.dynamic_slice_in_dim(ext_docs, first_row, row_count, 0) == own_docs
        live_mask = lax.dynamic_slice_in_dim(ext_live, first_row, row_count, 0)
        keep_mask = (same_doc & live_mask).astype(jnp.float32)[:, None]
        taps = lax.dynamic_index_in_dim(filter_bank, tap_index, 0, keepdims=False)
        return taps[None, :] * window * keep_mask

    short_sum = jnp.zeros(gated.shape, jnp.float32)
    for tap_index in range(short_filter.shape[0]):
        short_sum = short_sum + tap_term(tap_index, short_filter)

    def tap_block(block_index, partial_value):
        for offset in range(8):
            partial_value = partial_value + tap_term(block_index * 8 + offset, medium_filter)
        return partial_value

    medium_sum = lax.fori_loop(0, medium_taps // 8, tap_block, jnp.zeros(gated.shape, jnp.float32))
    mixed = queries * (short_sum + medium_sum + skip_gain[None, :] * gated.astype(jnp.float32))
    return mixed.astype(jnp.bfloat16)


def attention_mix(attn_query, attn_key, attn_value, lengths):
    row_count, col_count = attn_query.shape
    heads_here = col_count // HD
    span_index = lax.axis_index("seq")
    query_positions = span_index * row_count + jnp.arange(row_count, dtype=jnp.int32)
    query_docs = doc_of(query_positions, lengths)
    query_heads = attn_query.reshape(row_count, heads_here, HD)
    score_scale = HD ** (-0.5)
    last_query = query_positions[row_count - 1]
    first_query_doc = query_docs[0]

    def absorb(state_now, key_block, value_block, first_row):
        key_count = key_block.shape[0]
        last_key = first_row + key_count - 1
        last_key_doc = doc_of(jnp.reshape(last_key, (1,)), lengths)[0]
        masked_out = (first_row > last_query) | (last_key < 0) | (last_key_doc < first_query_doc)

        def compute(state_in):
            running_max, running_total, running_sum = state_in
            key_heads = key_block.reshape(key_count, heads_here, HD)
            value_heads = value_block.reshape(key_count, heads_here, HD)
            scores = (
                jnp.einsum(
                    "rhd,nhd->hrn", query_heads, key_heads, preferred_element_type=jnp.float32
                )
                * score_scale
            )
            key_positions = first_row + jnp.arange(key_count, dtype=jnp.int32)
            key_docs = doc_of(key_positions, lengths)
            allowed = (
                (key_positions[None, :] <= query_positions[:, None])
                & (key_docs[None, :] == query_docs[:, None])
                & (key_positions >= 0)[None, :]
            )
            masked = jnp.where(allowed[None], scores, -1e30)
            new_max = jnp.maximum(running_max, jnp.max(masked, axis=2))
            rescale = jnp.exp(running_max - new_max)
            weights = jnp.where(allowed[None], jnp.exp(scores - new_max[:, :, None]), 0.0)
            new_total = running_total * rescale + jnp.sum(weights, axis=2)
            product = jnp.einsum(
                "hrn,nhd->hrd",
                weights.astype(jnp.bfloat16),
                value_heads,
                preferred_element_type=jnp.float32,
            )
            new_sum = running_sum * rescale[:, :, None] + product
            return (new_max, new_total, new_sum)

        def keep_state(state_in):
            return state_in

        return lax.cond(masked_out, keep_state, compute, state_now)

    def fold_keys(state_now, pieces, first_row):
        key_all, value_all = pieces
        key_count = key_all.shape[0]
        block_rows = math.gcd(key_count, 1536)
        if block_rows == key_count:
            return absorb(state_now, key_all, value_all, first_row)
        block_total = key_count // block_rows
        key_blocks = key_all.reshape(block_total, block_rows, col_count)
        value_blocks = value_all.reshape(block_total, block_rows, col_count)

        def scan_step(state_inner, block_items):
            key_block, value_block, block_index = block_items
            return (
                absorb(state_inner, key_block, value_block, first_row + block_index * block_rows),
                None,
            )

        state_now, unused = lax.scan(
            scan_step,
            state_now,
            (key_blocks, value_blocks, jnp.arange(block_total, dtype=jnp.int32)),
        )
        return state_now

    initial = (
        jnp.full((heads_here, row_count), -1e30, jnp.float32),
        jnp.zeros((heads_here, row_count), jnp.float32),
        jnp.zeros((heads_here, row_count, HD), jnp.float32),
    )
    state_now = fold_keys(
        initial,
        (
            lax.all_gather(attn_key, "seq", axis=0, tiled=True),
            lax.all_gather(attn_value, "seq", axis=0, tiled=True),
        ),
        jnp.int32(0),
    )
    running_max, running_total, running_sum = state_now
    result = running_sum / running_total[:, :, None]
    return result.transpose(1, 0, 2).reshape(row_count, col_count).astype(jnp.bfloat16)


LOG2E = 1.4426950408889634
LN2 = 0.6931471805599453
SCALE2 = HD**-0.5 * LOG2E
NEG = -1e30
CHUNKS = 4
STAT_ROWS = 16


def hyena_kernel(row_count, rim, lens_ref, ext_in, query_ref, filt_ref, out_ref, ext_ref):
    base = lens_ref[lens_ref.shape[0] - 1]
    ext_ref[...] = ext_in[...]
    taps = filt_ref.shape[0]
    zero_row = jnp.zeros(ext_ref.shape[1:], ext_ref.dtype)
    start = jnp.int32(0)
    for doc in range(lens_ref.shape[0] - 1):
        end = start + lens_ref[doc]
        first = jnp.clip(start - base, -rim, row_count)
        last = jnp.clip(end - base, 0, row_count)

        @pl.when((last > 0) & (first < row_count) & (first < last))
        def _():
            def wipe(row, carry):
                ext_ref[row] = zero_row
                return carry

            lax.fori_loop(jnp.maximum(first, 0), first + rim, wipe, 0)
            tile_lo = jnp.maximum(first, 0) // 8
            tile_hi = (last + 7) // 8

            def tile_body(tile, carry):
                t0 = pl.multiple_of(tile * 8, 8)

                def tap_body(block, accs):
                    j0 = pl.multiple_of(block * 8, 8)
                    fs = [filt_ref[j0 + o] for o in range(8)]
                    low = t0 + rim - j0 - 7
                    gs = [ext_ref[low + o] for o in range(15)]
                    out = []
                    for i in range(8):
                        prods = [gs[i + 7 - o] * fs[o] for o in range(8)]
                        while len(prods) > 1:
                            prods = [a + b for a, b in zip(prods[::2], prods[1::2])]
                        out.append(accs[i] + prods[0].astype(jnp.float32))
                    return tuple(out)

                zeros = jnp.zeros(ext_ref.shape[1:], jnp.float32)
                accs = lax.fori_loop(0, taps // 8, tap_body, (zeros,) * 8)
                for i in range(8):
                    mixed = query_ref[t0 + i].astype(jnp.float32) * accs[i]

                    @pl.when(t0 + i >= first)
                    def _():
                        out_ref[t0 + i] = mixed.astype(out_ref.dtype)

                return carry

            lax.fori_loop(tile_lo, tile_hi, tile_body, 0)

        start = end


def hyena_fast(features, short_filter, medium_filter, skip_gain, lengths):
    row_count, _, cols = features.shape
    taps = medium_filter.shape[0]
    subs = cols // 128
    span_index = lax.axis_index("seq")
    gated = (features[:, 1].astype(jnp.float32) * features[:, 2].astype(jnp.float32)).astype(
        jnp.bfloat16
    )
    carried = passed_along(gated[row_count - taps :], "seq", 1)
    ext = jnp.concatenate((carried, gated), axis=0).reshape(row_count + taps, subs, 128)
    query = features[:, 0].reshape(row_count, subs, 128)
    filt = medium_filter.at[: short_filter.shape[0]].add(short_filter)
    filt = filt.at[0].add(skip_gain).astype(jnp.bfloat16).reshape(taps, subs, 128)
    scalars = jnp.concatenate((lengths, jnp.reshape(span_index * row_count, (1,)).astype(jnp.int32)))
    vmem = pl.BlockSpec(memory_space=pltpu.VMEM)
    out = pl.pallas_call(
        lambda *refs: hyena_kernel(row_count, taps, *refs),
        out_shape=jax.ShapeDtypeStruct((row_count, subs, 128), jnp.bfloat16),
        in_specs=[pl.BlockSpec(memory_space=pltpu.SMEM), vmem, vmem, vmem],
        out_specs=vmem,
        scratch_shapes=[pltpu.VMEM((row_count + taps, subs, 128), jnp.bfloat16)],
        compiler_params=pltpu.CompilerParams(vmem_limit_bytes=24 * 2**20),
        cost_estimate=pl.CostEstimate(
            flops=2 * taps * row_count * cols * 10, bytes_accessed=7 * 2**20, transcendentals=0
        ),
        name="hyena",
    )(scalars, ext, query, filt)
    return out.reshape(row_count, cols)


def doc_start(pos, lens_ref):
    start = jnp.zeros_like(pos)
    end = jnp.int32(0)
    for doc in range(lens_ref.shape[0] - 1):
        end = end + lens_ref[doc]
        start = jnp.where(pos >= end, end, start)
    return start


def attn_kernel(rows, lens_ref, q_ref, qa_ref, qb_ref, kp_ref, vp_ref, k_ref, v_ref,
                o_ref, lse_ref, oa_ref, ob_ref, b00, b10, b01, b11, b02):
    span = lens_ref[lens_ref.shape[0] - 1]
    base = span * rows

    def needs(ahead, back):
        q_first = base + ahead * rows
        start = jnp.int32(0)
        end = jnp.int32(0)
        for doc in range(lens_ref.shape[0] - 1):
            end = end + lens_ref[doc]
            start = jnp.where(q_first >= end, end, start)
        return start < base + (1 - back) * rows

    own_prev = (span == 1) & needs(0, 1)
    a_here = ((span == 1) | (span == 2)) & needs(1, 0)
    a_prev = (span == 1) & needs(1, 1)
    b_here = (span == 1) & needs(2, 0)

    @pl.when(pl.program_id(0) == 0)
    def _():
        def fill(ref, ahead, back):
            qpos = base + ahead * rows + lax.broadcasted_iota(jnp.int32, (rows, 1), 0)
            starts = doc_start(qpos, lens_ref)
            kpos = base - back * rows + lax.broadcasted_iota(jnp.int32, (1, rows), 1)
            ref[...] = jnp.where((kpos <= qpos) & (kpos >= starts), 0.0, NEG).astype(jnp.float32)

        fill(b00, 0, 0)
        pl.when(own_prev)(lambda: fill(b01, 0, 1))
        pl.when(a_here)(lambda: fill(b10, 1, 0))
        pl.when(a_prev)(lambda: fill(b11, 1, 1))
        pl.when(b_here)(lambda: fill(b02, 2, 0))

    step = 128
    ones = jnp.ones((rows, 128), jnp.bfloat16)

    def attend(query_ref, keys, values, biases, emit):
        vals = [jnp.concatenate((v[...], ones), axis=1) for v in values]
        for r in range(0, rows, step):
            q = query_ref[r : r + step, :]
            scores = [
                lax.dot_general(q, k[...], (((1,), (1,)), ((), ())),
                                preferred_element_type=jnp.float32) + b[r : r + step, :]
                for k, b in zip(keys, biases)
            ]
            top = jnp.max(scores[0], axis=1, keepdims=True)
            for s in scores[1:]:
                top = jnp.maximum(top, jnp.max(s, axis=1, keepdims=True))
            acc = None
            for s, v in zip(scores, vals):
                w = jnp.exp2((s - top) * SCALE2).astype(jnp.bfloat16)
                part = jnp.dot(w, v, preferred_element_type=jnp.float32)
                acc = part if acc is None else acc + part
            total = acc[:, 128:]
            emit(r, acc[:, :128] / total, top * SCALE2 + jnp.log2(total))

    def emit_own(r, out, lse):
        o_ref[r : r + step, :] = out
        lse_ref[r : r + step, :] = lse

    eye = lax.broadcasted_iota(jnp.int32, (128, 128), 0) == lax.broadcasted_iota(
        jnp.int32, (128, 128), 1
    )
    stat_iota = lax.broadcasted_iota(jnp.int32, (STAT_ROWS, 128), 0)

    def emit_to(ref):
        stats = [jnp.zeros((STAT_ROWS, 128), jnp.float32)]

        def emit(r, out, lse):
            ref[r : r + step, :] = out.astype(jnp.bfloat16)
            rest = jnp.sum(jnp.where(eye, lse, 0.0), axis=0, keepdims=True)
            for piece in range(3):
                high = rest.astype(jnp.bfloat16).astype(jnp.float32)
                stats[0] = jnp.where(stat_iota == piece * (rows // step) + r // step, high, stats[0])
                rest = rest - high
            if r + step == rows:
                ref[rows:, :] = stats[0].astype(jnp.bfloat16)

        return emit

    def empty(ref):
        ref[:rows, :] = jnp.zeros((rows, 128), jnp.bfloat16)
        ref[rows:, :] = jnp.where(stat_iota < rows // step, NEG, 0.0).astype(jnp.bfloat16)

    pl.when(own_prev)(lambda: attend(q_ref, (kp_ref, k_ref), (vp_ref, v_ref), (b01, b00), emit_own))
    pl.when(jnp.logical_not(own_prev))(lambda: attend(q_ref, (k_ref,), (v_ref,), (b00,), emit_own))
    pl.when(a_prev)(
        lambda: attend(qa_ref, (kp_ref, k_ref), (vp_ref, v_ref), (b11, b10), emit_to(oa_ref))
    )
    pl.when(a_here & jnp.logical_not(a_prev))(
        lambda: attend(qa_ref, (k_ref,), (v_ref,), (b10,), emit_to(oa_ref))
    )
    pl.when(jnp.logical_not(a_here))(lambda: empty(oa_ref))
    pl.when(b_here)(lambda: attend(qb_ref, (k_ref,), (v_ref,), (b02,), emit_to(ob_ref)))
    pl.when(jnp.logical_not(b_here))(lambda: empty(ob_ref))


def merge_kernel(rows, lens_ref, o_ref, lse_ref, ra_ref, rb_ref, out_ref):
    span = lens_ref[lens_ref.shape[0] - 1]
    step = 128
    eye = lax.broadcasted_iota(jnp.int32, (128, 128), 0) == lax.broadcasted_iota(
        jnp.int32, (128, 128), 1
    )

    @pl.when(span < 2)
    def _():
        out_ref[...] = o_ref[...].astype(jnp.bfloat16)

    @pl.when(span >= 2)
    def _():
        blocks = rows // step
        stat_a = ra_ref[rows:, :].astype(jnp.float32)
        stat_b = rb_ref[rows:, :].astype(jnp.float32)

        def column(stats, i):
            row = (stats[i : i + 1] + stats[blocks + i : blocks + i + 1]) + stats[
                2 * blocks + i : 2 * blocks + i + 1
            ]
            return jnp.sum(jnp.where(eye, row, 0.0), axis=1, keepdims=True)

        for i in range(blocks):
            r = i * step
            own = lse_ref[r : r + step, :]
            lse_a = column(stat_a, i)
            lse_b = jnp.where(span == 3, column(stat_b, i), NEG)
            top = jnp.maximum(own, jnp.maximum(lse_a, lse_b))
            w0 = jnp.exp2(own - top)
            w1 = jnp.exp2(lse_a - top)
            w2 = jnp.exp2(lse_b - top)
            total = (
                o_ref[r : r + step, :] * w0
                + ra_ref[r : r + step, :].astype(jnp.float32) * w1
                + rb_ref[r : r + step, :].astype(jnp.float32) * w2
            )
            out_ref[r : r + step, :] = (total / (w0 + w1 + w2)).astype(jnp.bfloat16)


def attention_fast(attn_query, attn_key, attn_value, lengths):
    rows, cols = attn_query.shape
    span_index = lax.axis_index("seq")
    scalars = jnp.concatenate((lengths, jnp.reshape(span_index, (1,)).astype(jnp.int32)))
    width = cols // CHUNKS
    heads = width // HD
    smem = pl.BlockSpec(memory_space=pltpu.SMEM)
    block = pl.BlockSpec((rows, HD), lambda h: (0, h))
    tall = pl.BlockSpec((rows + STAT_ROWS, HD), lambda h: (0, h))
    sent = []
    for c in range(CHUNKS):
        sl = slice(c * width, (c + 1) * width)
        qc, kc, vc = attn_query[:, sl], attn_key[:, sl], attn_value[:, sl]
        qa = lax.ppermute(qc, "seq", [(2, 1), (3, 2)])
        qb = lax.ppermute(qc, "seq", [(3, 1)])
        kp = lax.ppermute(kc, "seq", [(0, 1)])
        vp = lax.ppermute(vc, "seq", [(0, 1)])
        sent.append((qa, qb, kp, vp))
    outs = []
    for c in range(CHUNKS):
        qa, qb, kp, vp = sent[c]
        first = c * heads
        whole = pl.BlockSpec((rows, HD), lambda h, first=first: (0, first + h))
        own, lse, oa, ob = pl.pallas_call(
            lambda *refs: attn_kernel(rows, *refs),
            grid=(heads,),
            out_shape=(
                jax.ShapeDtypeStruct((rows, width), jnp.float32),
                jax.ShapeDtypeStruct((rows, width), jnp.float32),
                jax.ShapeDtypeStruct((rows + STAT_ROWS, width), jnp.bfloat16),
                jax.ShapeDtypeStruct((rows + STAT_ROWS, width), jnp.bfloat16),
            ),
            in_specs=[smem, whole, block, block, block, block, whole, whole],
            out_specs=(block, block, tall, tall),
            scratch_shapes=[pltpu.VMEM((rows, rows), jnp.float32)] * 5,
            compiler_params=pltpu.CompilerParams(vmem_limit_bytes=32 * 2**20),
            cost_estimate=pl.CostEstimate(
                flops=heads * 5 * rows * rows * HD * 4 * 2,
                bytes_accessed=8 * 2**20,
                transcendentals=heads * 5 * rows * rows,
            ),
            name="attend",
        )(scalars, attn_query, qa, qb, kp, vp, attn_key, attn_value)
        ra = lax.ppermute(oa, "seq", [(1, 2), (2, 3)])
        rb = lax.ppermute(ob, "seq", [(1, 3)])
        outs.append((own, lse, ra, rb))
    merged = []
    for own, lse, ra, rb in outs:
        merged.append(
            pl.pallas_call(
                lambda *refs: merge_kernel(rows, *refs),
                grid=(heads,),
                out_shape=jax.ShapeDtypeStruct((rows, width), jnp.bfloat16),
                in_specs=[smem, block, block, tall, tall],
                out_specs=block,
                cost_estimate=pl.CostEstimate(
                    flops=rows * width * 16, bytes_accessed=6 * 2**20, transcendentals=0
                ),
                name="merge",
            )(scalars, own, lse, ra, rb)
        )
    return jnp.concatenate(merged, axis=1)


def local(
    features, short_filter, medium_filter, skip_gain, attn_query, attn_key, attn_value, lengths
):
    rows, cols = attn_query.shape
    spans = lax.axis_size("seq")
    if cols % 2048 == 0 and rows % 8 == 0:
        hyena = hyena_fast
    else:
        hyena = hyena_mix
    if spans == 4 and rows % 128 == 0 and rows <= 640 and cols % (CHUNKS * HD) == 0:
        attention = attention_fast
    else:
        attention = attention_mix
    hyena_out = hyena(features, short_filter, medium_filter, skip_gain, lengths)
    attn_out = attention(attn_query, attn_key, attn_value, lengths)
    return (hyena_out, attn_out)


def solution(mesh):
    in_specs = (
        P(("groups", "seq"), None, ("tensor", "sub")),
        P(None, ("tensor", "sub")),
        P(None, ("tensor", "sub")),
        P(("tensor", "sub")),
        P(("groups", "seq"), ("tensor", "sub")),
        P(("groups", "seq"), ("tensor", "sub")),
        P(("groups", "seq"), ("tensor", "sub")),
        P("groups"),
    )
    out_specs = (P(("groups", "seq"), ("tensor", "sub")), P(("groups", "seq"), ("tensor", "sub")))
    return jax.shard_map(local, mesh=mesh, in_specs=in_specs, out_specs=out_specs, check_vma=False)
```

```python
import math

import jax
import jax.numpy as jnp
import numpy as np
from jax import lax
from jax.experimental import pallas as pl
from jax.experimental.pallas import tpu as pltpu
from jax.sharding import PartitionSpec as P

HD = 128


def passed_along(value, axis, by):
    length = lax.axis_size(axis)
    pairs = [(i, i + by) for i in range(length) if 0 <= i + by < length]
    return lax.ppermute(value, axis, pairs)


def doc_of(positions, lengths):
    doc_ends = jnp.cumsum(lengths, dtype=jnp.int32)
    return jnp.sum(
        (positions[:, None] >= doc_ends[None, :]).astype(jnp.int32), axis=1, dtype=jnp.int32
    )


def hyena_mix(features, short_filter, medium_filter, skip_gain, lengths):
    row_count = features.shape[0]
    medium_taps = medium_filter.shape[0]
    rim_rows = medium_taps - 1
    span_index = lax.axis_index("seq")
    queries = features[:, 0].astype(jnp.float32)
    gated = (features[:, 1].astype(jnp.float32) * features[:, 2].astype(jnp.float32)).astype(
        jnp.bfloat16
    )
    gated = lax.optimization_barrier(gated)
    carried = passed_along(gated[row_count - rim_rows :], "seq", 1)
    extended = jnp.concatenate((carried, gated), axis=0)
    ext_positions = (
        span_index * row_count - rim_rows + jnp.arange(row_count + rim_rows, dtype=jnp.int32)
    )
    ext_docs = doc_of(ext_positions, lengths)
    ext_live = ext_positions >= 0
    own_docs = ext_docs[rim_rows:]

    def tap_term(tap_index, filter_bank):
        first_row = rim_rows - tap_index
        window = lax.dynamic_slice_in_dim(extended, first_row, row_count, 0).astype(jnp.float32)
        same_doc = lax.dynamic_slice_in_dim(ext_docs, first_row, row_count, 0) == own_docs
        live_mask = lax.dynamic_slice_in_dim(ext_live, first_row, row_count, 0)
        keep_mask = (same_doc & live_mask).astype(jnp.float32)[:, None]
        taps = lax.dynamic_index_in_dim(filter_bank, tap_index, 0, keepdims=False)
        return taps[None, :] * window * keep_mask

    short_sum = jnp.zeros(gated.shape, jnp.float32)
    for tap_index in range(short_filter.shape[0]):
        short_sum = short_sum + tap_term(tap_index, short_filter)

    def tap_block(block_index, partial_value):
        for offset in range(8):
            partial_value = partial_value + tap_term(block_index * 8 + offset, medium_filter)
        return partial_value

    medium_sum = lax.fori_loop(0, medium_taps // 8, tap_block, jnp.zeros(gated.shape, jnp.float32))
    mixed = queries * (short_sum + medium_sum + skip_gain[None, :] * gated.astype(jnp.float32))
    return mixed.astype(jnp.bfloat16)


def attention_mix(attn_query, attn_key, attn_value, lengths):
    row_count, col_count = attn_query.shape
    heads_here = col_count // HD
    span_index = lax.axis_index("seq")
    query_positions = span_index * row_count + jnp.arange(row_count, dtype=jnp.int32)
    query_docs = doc_of(query_positions, lengths)
    query_heads = attn_query.reshape(row_count, heads_here, HD)
    score_scale = HD ** (-0.5)
    last_query = query_positions[row_count - 1]
    first_query_doc = query_docs[0]

    def absorb(state_now, key_block, value_block, first_row):
        key_count = key_block.shape[0]
        last_key = first_row + key_count - 1
        last_key_doc = doc_of(jnp.reshape(last_key, (1,)), lengths)[0]
        masked_out = (first_row > last_query) | (last_key < 0) | (last_key_doc < first_query_doc)

        def compute(state_in):
            running_max, running_total, running_sum = state_in
            key_heads = key_block.reshape(key_count, heads_here, HD)
            value_heads = value_block.reshape(key_count, heads_here, HD)
            scores = (
                jnp.einsum(
                    "rhd,nhd->hrn", query_heads, key_heads, preferred_element_type=jnp.float32
                )
                * score_scale
            )
            key_positions = first_row + jnp.arange(key_count, dtype=jnp.int32)
            key_docs = doc_of(key_positions, lengths)
            allowed = (
                (key_positions[None, :] <= query_positions[:, None])
                & (key_docs[None, :] == query_docs[:, None])
                & (key_positions >= 0)[None, :]
            )
            masked = jnp.where(allowed[None], scores, -1e30)
            new_max = jnp.maximum(running_max, jnp.max(masked, axis=2))
            rescale = jnp.exp(running_max - new_max)
            weights = jnp.where(allowed[None], jnp.exp(scores - new_max[:, :, None]), 0.0)
            new_total = running_total * rescale + jnp.sum(weights, axis=2)
            product = jnp.einsum(
                "hrn,nhd->hrd",
                weights.astype(jnp.bfloat16),
                value_heads,
                preferred_element_type=jnp.float32,
            )
            new_sum = running_sum * rescale[:, :, None] + product
            return (new_max, new_total, new_sum)

        def keep_state(state_in):
            return state_in

        return lax.cond(masked_out, keep_state, compute, state_now)

    def fold_keys(state_now, pieces, first_row):
        key_all, value_all = pieces
        key_count = key_all.shape[0]
        block_rows = math.gcd(key_count, 1536)
        if block_rows == key_count:
            return absorb(state_now, key_all, value_all, first_row)
        block_total = key_count // block_rows
        key_blocks = key_all.reshape(block_total, block_rows, col_count)
        value_blocks = value_all.reshape(block_total, block_rows, col_count)

        def scan_step(state_inner, block_items):
            key_block, value_block, block_index = block_items
            return (
                absorb(state_inner, key_block, value_block, first_row + block_index * block_rows),
                None,
            )

        state_now, unused = lax.scan(
            scan_step,
            state_now,
            (key_blocks, value_blocks, jnp.arange(block_total, dtype=jnp.int32)),
        )
        return state_now

    initial = (
        jnp.full((heads_here, row_count), -1e30, jnp.float32),
        jnp.zeros((heads_here, row_count), jnp.float32),
        jnp.zeros((heads_here, row_count, HD), jnp.float32),
    )
    state_now = fold_keys(
        initial,
        (
            lax.all_gather(attn_key, "seq", axis=0, tiled=True),
            lax.all_gather(attn_value, "seq", axis=0, tiled=True),
        ),
        jnp.int32(0),
    )
    running_max, running_total, running_sum = state_now
    result = running_sum / running_total[:, :, None]
    return result.transpose(1, 0, 2).reshape(row_count, col_count).astype(jnp.bfloat16)


LOG2E = 1.4426950408889634
LN2 = 0.6931471805599453
SCALE2 = HD**-0.5 * LOG2E
NEG = -1e30
CHUNKS = 2
STAT_ROWS = 16


def hyena_kernel(row_count, taps, lens_ref, feat_ref, rim_ref, filt_ref, fwd_ref, inv_ref, out_ref,
                 ext_ref, sum_ref):
    base = lens_ref[lens_ref.shape[0] - 1]
    ext_ref[:taps, :] = rim_ref[...]
    ext_ref[taps:, :] = (
        feat_ref[1].astype(jnp.float32) * feat_ref[2].astype(jnp.float32)
    ).astype(jnp.bfloat16)

    def dot(x, y):
        return jnp.dot(x, y, preferred_element_type=jnp.float32)

    filt = filt_ref[...]
    filt_hi = filt.astype(jnp.bfloat16)
    filt_lo = (filt - filt_hi.astype(jnp.float32)).astype(jnp.bfloat16)
    spec = (
        dot(fwd_ref[0, :, :taps], filt_hi)
        + dot(fwd_ref[1, :, :taps], filt_hi)
        + dot(fwd_ref[0, :, :taps], filt_lo)
    )
    spec_r, spec_i = spec[:taps], spec[taps:]
    win_iota = lax.broadcasted_iota(jnp.int32, (2 * taps, 1), 0)
    out_iota = lax.broadcasted_iota(jnp.int32, (taps, 1), 0)
    for block in range(row_count // taps):
        r0 = block * taps
        start = jnp.int32(0)
        for doc in range(lens_ref.shape[0] - 1):
            end = start + lens_ref[doc]
            first, last = start - base, end - base

            @pl.when((last > r0) & (first < r0 + taps) & (first < last))
            def _(first=first):
                window = ext_ref[r0 : r0 + 2 * taps, :]
                window = jnp.where(win_iota + (r0 - taps) >= first, window, jnp.zeros_like(window))
                wave = dot(fwd_ref[0], window) + dot(fwd_ref[1], window)
                wave_r, wave_i = wave[:taps], wave[taps:]
                prod = jnp.concatenate(
                    (
                        (wave_r * spec_r - wave_i * spec_i).astype(jnp.bfloat16),
                        (wave_r * spec_i + wave_i * spec_r).astype(jnp.bfloat16),
                    ),
                    axis=0,
                )
                sums = dot(inv_ref[0], prod) + dot(inv_ref[1], prod)
                sum_ref[...] = jnp.where(out_iota + r0 >= first, sums, sum_ref[...])

            start = end
        out_ref[r0 : r0 + taps, :] = (
            feat_ref[0, r0 : r0 + taps, :].astype(jnp.float32) * sum_ref[...]
        ).astype(out_ref.dtype)


def split_two(matrix):
    high = matrix.astype(jnp.bfloat16)
    low = (matrix - high.astype(np.float64)).astype(jnp.bfloat16)
    return np.stack((high, low))


def hyena_fast(features, short_filter, medium_filter, skip_gain, lengths):
    row_count, _, cols = features.shape
    taps = medium_filter.shape[0]
    span_index = lax.axis_index("seq")
    streams = features.transpose(1, 0, 2)
    tail = streams[:, row_count - taps :]
    gated_tail = (tail[1].astype(jnp.float32) * tail[2].astype(jnp.float32)).astype(jnp.bfloat16)
    carried = passed_along(gated_tail, "seq", 1)
    head = jnp.concatenate((short_filter[:1] + skip_gain[None, :], short_filter[1:]), axis=0)
    filt = medium_filter + jnp.pad(head, ((0, taps - head.shape[0]), (0, 0)))
    angle = np.pi / (2 * taps) * np.outer(2 * np.arange(taps) + 1, np.arange(2 * taps))
    fwd = split_two(np.concatenate((np.cos(angle), -np.sin(angle)), axis=0))
    inv = split_two(
        np.concatenate((np.cos(angle), -np.sin(angle)), axis=0).T[taps:] / taps
    )
    scalars = jnp.concatenate((lengths, jnp.reshape(span_index * row_count, (1,)).astype(jnp.int32)))
    width = math.gcd(cols, 512)
    return pl.pallas_call(
        lambda *refs: hyena_kernel(row_count, taps, *refs),
        grid=(cols // width,),
        out_shape=jax.ShapeDtypeStruct((row_count, cols), jnp.bfloat16),
        in_specs=[
            pl.BlockSpec(memory_space=pltpu.SMEM),
            pl.BlockSpec((3, row_count, width), lambda i: (0, 0, i)),
            pl.BlockSpec((taps, width), lambda i: (0, i)),
            pl.BlockSpec((taps, width), lambda i: (0, i)),
            pl.BlockSpec(fwd.shape, lambda i: (0, 0, 0)),
            pl.BlockSpec(inv.shape, lambda i: (0, 0, 0)),
        ],
        out_specs=pl.BlockSpec((row_count, width), lambda i: (0, i)),
        scratch_shapes=[
            pltpu.VMEM((row_count + taps, width), jnp.bfloat16),
            pltpu.VMEM((taps, width), jnp.float32),
        ],
        compiler_params=pltpu.CompilerParams(vmem_limit_bytes=32 * 2**20),
        cost_estimate=pl.CostEstimate(
            flops=2 * 9 * 2 * taps * taps * 3 * cols, bytes_accessed=8 * 2**20, transcendentals=0
        ),
        name="hyena",
    )(scalars, streams, carried, filt, fwd, inv)


def doc_start(pos, lens_ref):
    start = jnp.zeros_like(pos)
    end = jnp.int32(0)
    for doc in range(lens_ref.shape[0] - 1):
        end = end + lens_ref[doc]
        start = jnp.where(pos >= end, end, start)
    return start


def attn_kernel(rows, lens_ref, q_ref, qa_ref, qb_ref, kp_ref, vp_ref, k_ref, v_ref,
                o_ref, lse_ref, oa_ref, ob_ref, b00, b10, b01, b11, b02):
    span = lens_ref[lens_ref.shape[0] - 1]
    base = span * rows

    def needs(ahead, back):
        q_first = base + ahead * rows
        start = jnp.int32(0)
        end = jnp.int32(0)
        for doc in range(lens_ref.shape[0] - 1):
            end = end + lens_ref[doc]
            start = jnp.where(q_first >= end, end, start)
        return start < base + (1 - back) * rows

    own_prev = (span == 1) & needs(0, 1)
    a_here = ((span == 1) | (span == 2)) & needs(1, 0)
    a_prev = (span == 1) & needs(1, 1)
    b_here = (span == 1) & needs(2, 0)

    @pl.when(pl.program_id(0) == 0)
    def _():
        def fill(ref, ahead, back):
            qpos = base + ahead * rows + lax.broadcasted_iota(jnp.int32, (rows, 1), 0)
            starts = doc_start(qpos, lens_ref)
            kpos = base - back * rows + lax.broadcasted_iota(jnp.int32, (1, rows), 1)
            ref[...] = jnp.where((kpos <= qpos) & (kpos >= starts), 0.0, NEG).astype(jnp.float32)

        fill(b00, 0, 0)
        pl.when(own_prev)(lambda: fill(b01, 0, 1))
        pl.when(a_here)(lambda: fill(b10, 1, 0))
        pl.when(a_prev)(lambda: fill(b11, 1, 1))
        pl.when(b_here)(lambda: fill(b02, 2, 0))

    step = 128
    ones = jnp.ones((rows, 128), jnp.bfloat16)

    def attend(query_ref, keys, values, biases, emit):
        vals = [jnp.concatenate((v[...], ones), axis=1) for v in values]
        for r in range(0, rows, step):
            q = query_ref[r : r + step, :]
            scores = [
                lax.dot_general(q, k[...], (((1,), (1,)), ((), ())),
                                preferred_element_type=jnp.float32) + b[r : r + step, :]
                for k, b in zip(keys, biases)
            ]
            top = jnp.max(scores[0], axis=1, keepdims=True)
            for s in scores[1:]:
                top = jnp.maximum(top, jnp.max(s, axis=1, keepdims=True))
            acc = None
            for s, v in zip(scores, vals):
                w = jnp.exp2((s - top) * SCALE2).astype(jnp.bfloat16)
                part = jnp.dot(w, v, preferred_element_type=jnp.float32)
                acc = part if acc is None else acc + part
            total = acc[:, 128:]
            emit(r, acc[:, :128] / total, top * SCALE2 + jnp.log2(total))

    def emit_own(r, out, lse):
        o_ref[r : r + step, :] = out
        lse_ref[r : r + step, :] = lse

    eye = lax.broadcasted_iota(jnp.int32, (128, 128), 0) == lax.broadcasted_iota(
        jnp.int32, (128, 128), 1
    )
    stat_iota = lax.broadcasted_iota(jnp.int32, (STAT_ROWS, 128), 0)

    def emit_to(ref):
        stats = [jnp.zeros((STAT_ROWS, 128), jnp.float32)]

        def emit(r, out, lse):
            ref[r : r + step, :] = out.astype(jnp.bfloat16)
            rest = jnp.sum(jnp.where(eye, lse, 0.0), axis=0, keepdims=True)
            for piece in range(3):
                high = rest.astype(jnp.bfloat16).astype(jnp.float32)
                stats[0] = jnp.where(stat_iota == piece * (rows // step) + r // step, high, stats[0])
                rest = rest - high
            if r + step == rows:
                ref[rows:, :] = stats[0].astype(jnp.bfloat16)

        return emit

    def empty(ref):
        ref[:rows, :] = jnp.zeros((rows, 128), jnp.bfloat16)
        ref[rows:, :] = jnp.where(stat_iota < rows // step, NEG, 0.0).astype(jnp.bfloat16)

    pl.when(own_prev)(lambda: attend(q_ref, (kp_ref, k_ref), (vp_ref, v_ref), (b01, b00), emit_own))
    pl.when(jnp.logical_not(own_prev))(lambda: attend(q_ref, (k_ref,), (v_ref,), (b00,), emit_own))
    pl.when(a_prev)(
        lambda: attend(qa_ref, (kp_ref, k_ref), (vp_ref, v_ref), (b11, b10), emit_to(oa_ref))
    )
    pl.when(a_here & jnp.logical_not(a_prev))(
        lambda: attend(qa_ref, (k_ref,), (v_ref,), (b10,), emit_to(oa_ref))
    )
    pl.when(jnp.logical_not(a_here))(lambda: empty(oa_ref))
    pl.when(b_here)(lambda: attend(qb_ref, (k_ref,), (v_ref,), (b02,), emit_to(ob_ref)))
    pl.when(jnp.logical_not(b_here))(lambda: empty(ob_ref))


def merge_kernel(rows, lens_ref, o_ref, lse_ref, ra_ref, rb_ref, out_ref):
    span = lens_ref[lens_ref.shape[0] - 1]
    step = 128
    eye = lax.broadcasted_iota(jnp.int32, (128, 128), 0) == lax.broadcasted_iota(
        jnp.int32, (128, 128), 1
    )

    @pl.when(span < 2)
    def _():
        out_ref[...] = o_ref[...].astype(jnp.bfloat16)

    @pl.when(span >= 2)
    def _():
        blocks = rows // step
        stat_a = ra_ref[rows:, :].astype(jnp.float32)
        stat_b = rb_ref[rows:, :].astype(jnp.float32)

        def column(stats, i):
            row = (stats[i : i + 1] + stats[blocks + i : blocks + i + 1]) + stats[
                2 * blocks + i : 2 * blocks + i + 1
            ]
            return jnp.sum(jnp.where(eye, row, 0.0), axis=1, keepdims=True)

        for i in range(blocks):
            r = i * step
            own = lse_ref[r : r + step, :]
            lse_a = column(stat_a, i)
            lse_b = jnp.where(span == 3, column(stat_b, i), NEG)
            top = jnp.maximum(own, jnp.maximum(lse_a, lse_b))
            w0 = jnp.exp2(own - top)
            w1 = jnp.exp2(lse_a - top)
            w2 = jnp.exp2(lse_b - top)
            total = (
                o_ref[r : r + step, :] * w0
                + ra_ref[r : r + step, :].astype(jnp.float32) * w1
                + rb_ref[r : r + step, :].astype(jnp.float32) * w2
            )
            out_ref[r : r + step, :] = (total / (w0 + w1 + w2)).astype(jnp.bfloat16)


def attention_fast(attn_query, attn_key, attn_value, lengths, hyena_out):
    rows, cols = attn_query.shape
    span_index = lax.axis_index("seq")
    scalars = jnp.concatenate((lengths, jnp.reshape(span_index, (1,)).astype(jnp.int32)))
    width = cols // CHUNKS
    heads = width // HD
    smem = pl.BlockSpec(memory_space=pltpu.SMEM)
    block = pl.BlockSpec((rows, HD), lambda h: (0, h))
    tall = pl.BlockSpec((rows + STAT_ROWS, HD), lambda h: (0, h))
    sent = []
    for c in range(CHUNKS):
        sl = slice(c * width, (c + 1) * width)
        qc = attn_query[:, sl]
        kv = jnp.concatenate((attn_key[:, sl], attn_value[:, sl]), axis=1)
        qa = lax.ppermute(qc, "seq", [(2, 1), (3, 2)])
        qb = lax.ppermute(qc, "seq", [(3, 1)])
        sent.append((qa, qb, lax.ppermute(kv, "seq", [(0, 1)])))
    scalars, hyena_out = lax.optimization_barrier((scalars, hyena_out))
    other = pl.BlockSpec((rows, HD), lambda h: (0, heads + h))
    outs = []
    for c in range(CHUNKS):
        qa, qb, kvp = sent[c]
        first = c * heads
        whole = pl.BlockSpec((rows, HD), lambda h, first=first: (0, first + h))
        own, lse, oa, ob = pl.pallas_call(
            lambda *refs: attn_kernel(rows, *refs),
            grid=(heads,),
            out_shape=(
                jax.ShapeDtypeStruct((rows, width), jnp.float32),
                jax.ShapeDtypeStruct((rows, width), jnp.float32),
                jax.ShapeDtypeStruct((rows + STAT_ROWS, width), jnp.bfloat16),
                jax.ShapeDtypeStruct((rows + STAT_ROWS, width), jnp.bfloat16),
            ),
            in_specs=[smem, whole, block, block, block, other, whole, whole],
            out_specs=(block, block, tall, tall),
            scratch_shapes=[pltpu.VMEM((rows, rows), jnp.float32)] * 5,
            compiler_params=pltpu.CompilerParams(vmem_limit_bytes=32 * 2**20),
            cost_estimate=pl.CostEstimate(
                flops=heads * 5 * rows * rows * HD * 4 * 2,
                bytes_accessed=8 * 2**20,
                transcendentals=heads * 5 * rows * rows,
            ),
            name="attend",
        )(scalars, attn_query, qa, qb, kvp, kvp, attn_key, attn_value)
        ra = lax.ppermute(oa, "seq", [(1, 2), (2, 3)])
        rb = lax.ppermute(ob, "seq", [(1, 3)])
        outs.append((own, lse, ra, rb))
    merged = []
    for own, lse, ra, rb in outs:
        merged.append(
            pl.pallas_call(
                lambda *refs: merge_kernel(rows, *refs),
                grid=(heads,),
                out_shape=jax.ShapeDtypeStruct((rows, width), jnp.bfloat16),
                in_specs=[smem, block, block, tall, tall],
                out_specs=block,
                cost_estimate=pl.CostEstimate(
                    flops=rows * width * 16, bytes_accessed=6 * 2**20, transcendentals=0
                ),
                name="merge",
            )(scalars, own, lse, ra, rb)
        )
    return hyena_out, jnp.concatenate(merged, axis=1)


def local(
    features, short_filter, medium_filter, skip_gain, attn_query, attn_key, attn_value, lengths
):
    rows, cols = attn_query.shape
    spans = lax.axis_size("seq")
    taps = medium_filter.shape[0]
    if cols % 128 == 0 and taps % 128 == 0 and rows % taps == 0:
        hyena = hyena_fast
    else:
        hyena = hyena_mix
    hyena_out = hyena(features, short_filter, medium_filter, skip_gain, lengths)
    if spans == 4 and rows % 128 == 0 and rows <= 640 and cols % (CHUNKS * HD) == 0:
        return attention_fast(attn_query, attn_key, attn_value, lengths, hyena_out)
    return (hyena_out, attention_mix(attn_query, attn_key, attn_value, lengths))


def solution(mesh):
    in_specs = (
        P(("groups", "seq"), None, ("tensor", "sub")),
        P(None, ("tensor", "sub")),
        P(None, ("tensor", "sub")),
        P(("tensor", "sub")),
        P(("groups", "seq"), ("tensor", "sub")),
        P(("groups", "seq"), ("tensor", "sub")),
        P(("groups", "seq"), ("tensor", "sub")),
        P("groups"),
    )
    out_specs = (P(("groups", "seq"), ("tensor", "sub")), P(("groups", "seq"), ("tensor", "sub")))
    return jax.shard_map(local, mesh=mesh, in_specs=in_specs, out_specs=out_specs, check_vma=False)
```

```python
import math

import jax
import jax.numpy as jnp
import numpy as np
from jax import lax
from jax.experimental import pallas as pl
from jax.experimental.pallas import tpu as pltpu
from jax.sharding import PartitionSpec as P

HD = 128


def passed_along(value, axis, by):
    length = lax.axis_size(axis)
    pairs = [(i, i + by) for i in range(length) if 0 <= i + by < length]
    return lax.ppermute(value, axis, pairs)


def doc_of(positions, lengths):
    doc_ends = jnp.cumsum(lengths, dtype=jnp.int32)
    return jnp.sum(
        (positions[:, None] >= doc_ends[None, :]).astype(jnp.int32), axis=1, dtype=jnp.int32
    )


def hyena_mix(features, short_filter, medium_filter, skip_gain, lengths):
    row_count = features.shape[0]
    medium_taps = medium_filter.shape[0]
    rim_rows = medium_taps - 1
    span_index = lax.axis_index("seq")
    queries = features[:, 0].astype(jnp.float32)
    gated = (features[:, 1].astype(jnp.float32) * features[:, 2].astype(jnp.float32)).astype(
        jnp.bfloat16
    )
    gated = lax.optimization_barrier(gated)
    carried = passed_along(gated[row_count - rim_rows :], "seq", 1)
    extended = jnp.concatenate((carried, gated), axis=0)
    ext_positions = (
        span_index * row_count - rim_rows + jnp.arange(row_count + rim_rows, dtype=jnp.int32)
    )
    ext_docs = doc_of(ext_positions, lengths)
    ext_live = ext_positions >= 0
    own_docs = ext_docs[rim_rows:]

    def tap_term(tap_index, filter_bank):
        first_row = rim_rows - tap_index
        window = lax.dynamic_slice_in_dim(extended, first_row, row_count, 0).astype(jnp.float32)
        same_doc = lax.dynamic_slice_in_dim(ext_docs, first_row, row_count, 0) == own_docs
        live_mask = lax.dynamic_slice_in_dim(ext_live, first_row, row_count, 0)
        keep_mask = (same_doc & live_mask).astype(jnp.float32)[:, None]
        taps = lax.dynamic_index_in_dim(filter_bank, tap_index, 0, keepdims=False)
        return taps[None, :] * window * keep_mask

    short_sum = jnp.zeros(gated.shape, jnp.float32)
    for tap_index in range(short_filter.shape[0]):
        short_sum = short_sum + tap_term(tap_index, short_filter)

    def tap_block(block_index, partial_value):
        for offset in range(8):
            partial_value = partial_value + tap_term(block_index * 8 + offset, medium_filter)
        return partial_value

    medium_sum = lax.fori_loop(0, medium_taps // 8, tap_block, jnp.zeros(gated.shape, jnp.float32))
    mixed = queries * (short_sum + medium_sum + skip_gain[None, :] * gated.astype(jnp.float32))
    return mixed.astype(jnp.bfloat16)


def attention_mix(attn_query, attn_key, attn_value, lengths):
    row_count, col_count = attn_query.shape
    heads_here = col_count // HD
    span_index = lax.axis_index("seq")
    query_positions = span_index * row_count + jnp.arange(row_count, dtype=jnp.int32)
    query_docs = doc_of(query_positions, lengths)
    query_heads = attn_query.reshape(row_count, heads_here, HD)
    score_scale = HD ** (-0.5)
    last_query = query_positions[row_count - 1]
    first_query_doc = query_docs[0]

    def absorb(state_now, key_block, value_block, first_row):
        key_count = key_block.shape[0]
        last_key = first_row + key_count - 1
        last_key_doc = doc_of(jnp.reshape(last_key, (1,)), lengths)[0]
        masked_out = (first_row > last_query) | (last_key < 0) | (last_key_doc < first_query_doc)

        def compute(state_in):
            running_max, running_total, running_sum = state_in
            key_heads = key_block.reshape(key_count, heads_here, HD)
            value_heads = value_block.reshape(key_count, heads_here, HD)
            scores = (
                jnp.einsum(
                    "rhd,nhd->hrn", query_heads, key_heads, preferred_element_type=jnp.float32
                )
                * score_scale
            )
            key_positions = first_row + jnp.arange(key_count, dtype=jnp.int32)
            key_docs = doc_of(key_positions, lengths)
            allowed = (
                (key_positions[None, :] <= query_positions[:, None])
                & (key_docs[None, :] == query_docs[:, None])
                & (key_positions >= 0)[None, :]
            )
            masked = jnp.where(allowed[None], scores, -1e30)
            new_max = jnp.maximum(running_max, jnp.max(masked, axis=2))
            rescale = jnp.exp(running_max - new_max)
            weights = jnp.where(allowed[None], jnp.exp(scores - new_max[:, :, None]), 0.0)
            new_total = running_total * rescale + jnp.sum(weights, axis=2)
            product = jnp.einsum(
                "hrn,nhd->hrd",
                weights.astype(jnp.bfloat16),
                value_heads,
                preferred_element_type=jnp.float32,
            )
            new_sum = running_sum * rescale[:, :, None] + product
            return (new_max, new_total, new_sum)

        def keep_state(state_in):
            return state_in

        return lax.cond(masked_out, keep_state, compute, state_now)

    def fold_keys(state_now, pieces, first_row):
        key_all, value_all = pieces
        key_count = key_all.shape[0]
        block_rows = math.gcd(key_count, 1536)
        if block_rows == key_count:
            return absorb(state_now, key_all, value_all, first_row)
        block_total = key_count // block_rows
        key_blocks = key_all.reshape(block_total, block_rows, col_count)
        value_blocks = value_all.reshape(block_total, block_rows, col_count)

        def scan_step(state_inner, block_items):
            key_block, value_block, block_index = block_items
            return (
                absorb(state_inner, key_block, value_block, first_row + block_index * block_rows),
                None,
            )

        state_now, unused = lax.scan(
            scan_step,
            state_now,
            (key_blocks, value_blocks, jnp.arange(block_total, dtype=jnp.int32)),
        )
        return state_now

    initial = (
        jnp.full((heads_here, row_count), -1e30, jnp.float32),
        jnp.zeros((heads_here, row_count), jnp.float32),
        jnp.zeros((heads_here, row_count, HD), jnp.float32),
    )
    state_now = fold_keys(
        initial,
        (
            lax.all_gather(attn_key, "seq", axis=0, tiled=True),
            lax.all_gather(attn_value, "seq", axis=0, tiled=True),
        ),
        jnp.int32(0),
    )
    running_max, running_total, running_sum = state_now
    result = running_sum / running_total[:, :, None]
    return result.transpose(1, 0, 2).reshape(row_count, col_count).astype(jnp.bfloat16)


LOG2E = 1.4426950408889634
LN2 = 0.6931471805599453
SCALE2 = HD**-0.5 * LOG2E
NEG = -1e30
STAT_ROWS = 16


def hyena_kernel(row_count, taps, lens_ref, feat_ref, rim_ref, filt_ref, fwd_ref, inv_ref, out_ref,
                 ext_ref, sum_ref):
    base = lens_ref[lens_ref.shape[0] - 1]
    ext_ref[:taps, :] = rim_ref[...]
    ext_ref[taps:, :] = (
        feat_ref[1].astype(jnp.float32) * feat_ref[2].astype(jnp.float32)
    ).astype(jnp.bfloat16)

    def dot(x, y):
        return jnp.dot(x, y, preferred_element_type=jnp.float32)

    filt = filt_ref[...]
    filt_hi = filt.astype(jnp.bfloat16)
    filt_lo = (filt - filt_hi.astype(jnp.float32)).astype(jnp.bfloat16)
    spec = (
        dot(fwd_ref[0, :, :taps], filt_hi)
        + dot(fwd_ref[1, :, :taps], filt_hi)
        + dot(fwd_ref[0, :, :taps], filt_lo)
    )
    spec_r, spec_i = spec[:taps], spec[taps:]
    win_iota = lax.broadcasted_iota(jnp.int32, (2 * taps, 1), 0)
    out_iota = lax.broadcasted_iota(jnp.int32, (taps, 1), 0)
    for block in range(row_count // taps):
        r0 = block * taps
        start = jnp.int32(0)
        for doc in range(lens_ref.shape[0] - 1):
            end = start + lens_ref[doc]
            first, last = start - base, end - base

            @pl.when((last > r0) & (first < r0 + taps) & (first < last))
            def _(first=first):
                window = ext_ref[r0 : r0 + 2 * taps, :]
                window = jnp.where(win_iota + (r0 - taps) >= first, window, jnp.zeros_like(window))
                wave = dot(fwd_ref[0], window) + dot(fwd_ref[1], window)
                wave_r, wave_i = wave[:taps], wave[taps:]
                prod = jnp.concatenate(
                    (
                        (wave_r * spec_r - wave_i * spec_i).astype(jnp.bfloat16),
                        (wave_r * spec_i + wave_i * spec_r).astype(jnp.bfloat16),
                    ),
                    axis=0,
                )
                sums = dot(inv_ref[0], prod) + dot(inv_ref[1], prod)
                sum_ref[...] = jnp.where(out_iota + r0 >= first, sums, sum_ref[...])

            start = end
        out_ref[r0 : r0 + taps, :] = (
            feat_ref[0, r0 : r0 + taps, :].astype(jnp.float32) * sum_ref[...]
        ).astype(out_ref.dtype)


def split_two(matrix):
    high = matrix.astype(jnp.bfloat16)
    low = (matrix - high.astype(np.float64)).astype(jnp.bfloat16)
    return np.stack((high, low))


def hyena_fast(features, short_filter, medium_filter, skip_gain, lengths):
    row_count, _, cols = features.shape
    taps = medium_filter.shape[0]
    span_index = lax.axis_index("seq")
    streams = features.transpose(1, 0, 2)
    tail = streams[:, row_count - taps :]
    gated_tail = (tail[1].astype(jnp.float32) * tail[2].astype(jnp.float32)).astype(jnp.bfloat16)
    carried = passed_along(gated_tail, "seq", 1)
    head = jnp.concatenate((short_filter[:1] + skip_gain[None, :], short_filter[1:]), axis=0)
    filt = medium_filter + jnp.pad(head, ((0, taps - head.shape[0]), (0, 0)))
    angle = np.pi / (2 * taps) * np.outer(2 * np.arange(taps) + 1, np.arange(2 * taps))
    fwd = split_two(np.concatenate((np.cos(angle), -np.sin(angle)), axis=0))
    inv = split_two(
        np.concatenate((np.cos(angle), -np.sin(angle)), axis=0).T[taps:] / taps
    )
    scalars = jnp.concatenate((lengths, jnp.reshape(span_index * row_count, (1,)).astype(jnp.int32)))
    width = math.gcd(cols, 512)
    return pl.pallas_call(
        lambda *refs: hyena_kernel(row_count, taps, *refs),
        grid=(cols // width,),
        out_shape=jax.ShapeDtypeStruct((row_count, cols), jnp.bfloat16),
        in_specs=[
            pl.BlockSpec(memory_space=pltpu.SMEM),
            pl.BlockSpec((3, row_count, width), lambda i: (0, 0, i)),
            pl.BlockSpec((taps, width), lambda i: (0, i)),
            pl.BlockSpec((taps, width), lambda i: (0, i)),
            pl.BlockSpec(fwd.shape, lambda i: (0, 0, 0)),
            pl.BlockSpec(inv.shape, lambda i: (0, 0, 0)),
        ],
        out_specs=pl.BlockSpec((row_count, width), lambda i: (0, i)),
        scratch_shapes=[
            pltpu.VMEM((row_count + taps, width), jnp.bfloat16),
            pltpu.VMEM((taps, width), jnp.float32),
        ],
        compiler_params=pltpu.CompilerParams(vmem_limit_bytes=32 * 2**20),
        cost_estimate=pl.CostEstimate(
            flops=2 * 9 * 2 * taps * taps * 3 * cols, bytes_accessed=8 * 2**20, transcendentals=0
        ),
        name="hyena",
    )(scalars, streams, carried, filt, fwd, inv)


def doc_start(pos, lens_ref):
    start = jnp.zeros_like(pos)
    end = jnp.int32(0)
    for doc in range(lens_ref.shape[0] - 1):
        end = end + lens_ref[doc]
        start = jnp.where(pos >= end, end, start)
    return start


def attend(query_ref, keys, values, biases, emit):
    rows = query_ref.shape[0]
    step = 128
    ones = jnp.ones((rows, 128), jnp.bfloat16)
    vals = [jnp.concatenate((v[...], ones), axis=1) for v in values]
    for r in range(0, rows, step):
        q = query_ref[r : r + step, :]
        scores = [
            lax.dot_general(q, k[...], (((1,), (1,)), ((), ())),
                            preferred_element_type=jnp.float32) + b[r : r + step, :]
            for k, b in zip(keys, biases)
        ]
        top = jnp.max(scores[0], axis=1, keepdims=True)
        for s in scores[1:]:
            top = jnp.maximum(top, jnp.max(s, axis=1, keepdims=True))
        acc = None
        for s, v in zip(scores, vals):
            w = jnp.exp2((s - top) * SCALE2).astype(jnp.bfloat16)
            part = jnp.dot(w, v, preferred_element_type=jnp.float32)
            acc = part if acc is None else acc + part
        total = acc[:, 128:]
        emit(r, acc[:, :128] / total, top * SCALE2 + jnp.log2(total))


def needs(lens_ref, base, rows, ahead, back):
    q_first = base + ahead * rows
    start = jnp.int32(0)
    end = jnp.int32(0)
    for doc in range(lens_ref.shape[0] - 1):
        end = end + lens_ref[doc]
        start = jnp.where(q_first >= end, end, start)
    return start < base + (1 - back) * rows


def fill_bias(lens_ref, base, rows, ref, ahead, back):
    qpos = base + ahead * rows + lax.broadcasted_iota(jnp.int32, (rows, 1), 0)
    starts = doc_start(qpos, lens_ref)
    kpos = base - back * rows + lax.broadcasted_iota(jnp.int32, (1, rows), 1)
    ref[...] = jnp.where((kpos <= qpos) & (kpos >= starts), 0.0, NEG).astype(jnp.float32)


def near_kernel(rows, lens_ref, q_ref, k_ref, v_ref, k1_ref, v1_ref, k2_ref, v2_ref, all_ref, o_ref,
                b0, b1, b2):
    span = lens_ref[lens_ref.shape[0] - 1]
    base = span * rows
    one = (span >= 1) & needs(lens_ref, base, rows, 0, 1)
    two = (span >= 2) & needs(lens_ref, base, rows, 0, 2)

    @pl.when(pl.program_id(0) == 0)
    def _():
        fill_bias(lens_ref, base, rows, b0, 0, 0)
        pl.when(one)(lambda: fill_bias(lens_ref, base, rows, b1, 0, 1))
        pl.when(two)(lambda: fill_bias(lens_ref, base, rows, b2, 0, 2))

    def emit(r, out, lse):
        o_ref[r : r + 128, :] = out.astype(jnp.bfloat16)

    pl.when(two)(
        lambda: attend(q_ref, (k_ref, k1_ref, k2_ref), (v_ref, v1_ref, v2_ref), (b0, b1, b2), emit)
    )
    pl.when(one & jnp.logical_not(two))(
        lambda: attend(q_ref, (k_ref, k1_ref), (v_ref, v1_ref), (b0, b1), emit)
    )
    pl.when(jnp.logical_not(one))(lambda: attend(q_ref, (k_ref,), (v_ref,), (b0,), emit))


def attn_kernel(rows, lens_ref, q_ref, qa_ref, qb_ref, kp_ref, vp_ref, k_ref, v_ref,
                o_ref, lse_ref, oa_ref, ob_ref, b00, b10, b01, b11, b02):
    span = lens_ref[lens_ref.shape[0] - 1]
    base = span * rows

    def reads(ahead, back):
        return needs(lens_ref, base, rows, ahead, back)

    own_prev = (span == 1) & reads(0, 1)
    a_here = ((span == 1) | (span == 2)) & reads(1, 0)
    a_prev = (span == 1) & reads(1, 1)
    b_here = (span == 1) & reads(2, 0)

    @pl.when(pl.program_id(0) == 0)
    def _():
        lse_ref[...] = jnp.zeros_like(lse_ref)

        def fill(ref, ahead, back):
            fill_bias(lens_ref, base, rows, ref, ahead, back)

        fill(b00, 0, 0)
        pl.when(own_prev)(lambda: fill(b01, 0, 1))
        pl.when(a_here)(lambda: fill(b10, 1, 0))
        pl.when(a_prev)(lambda: fill(b11, 1, 1))
        pl.when(b_here)(lambda: fill(b02, 2, 0))

    step = 128
    head_lane = lax.broadcasted_iota(jnp.int32, (step, 128), 1) == pl.program_id(0)

    def emit_own(r, out, lse):
        o_ref[r : r + step, :] = out.astype(jnp.bfloat16)
        lse_ref[r : r + step, :] = jnp.where(head_lane, lse, lse_ref[r : r + step, :])

    eye = lax.broadcasted_iota(jnp.int32, (128, 128), 0) == lax.broadcasted_iota(
        jnp.int32, (128, 128), 1
    )
    stat_iota = lax.broadcasted_iota(jnp.int32, (STAT_ROWS, 128), 0)

    def emit_to(ref):
        stats = [jnp.zeros((STAT_ROWS, 128), jnp.float32)]

        def emit(r, out, lse):
            ref[r : r + step, :] = out.astype(jnp.bfloat16)
            rest = jnp.sum(jnp.where(eye, lse, 0.0), axis=0, keepdims=True)
            for piece in range(3):
                high = rest.astype(jnp.bfloat16).astype(jnp.float32)
                stats[0] = jnp.where(stat_iota == piece * (rows // step) + r // step, high, stats[0])
                rest = rest - high
            if r + step == rows:
                ref[rows:, :] = stats[0].astype(jnp.bfloat16)

        return emit

    def empty(ref):
        ref[:rows, :] = jnp.zeros((rows, 128), jnp.bfloat16)
        ref[rows:, :] = jnp.where(stat_iota < rows // step, NEG, 0.0).astype(jnp.bfloat16)

    pl.when(own_prev)(lambda: attend(q_ref, (kp_ref, k_ref), (vp_ref, v_ref), (b01, b00), emit_own))
    pl.when(jnp.logical_not(own_prev))(lambda: attend(q_ref, (k_ref,), (v_ref,), (b00,), emit_own))
    pl.when(a_prev)(
        lambda: attend(qa_ref, (kp_ref, k_ref), (vp_ref, v_ref), (b11, b10), emit_to(oa_ref))
    )
    pl.when(a_here & jnp.logical_not(a_prev))(
        lambda: attend(qa_ref, (k_ref,), (v_ref,), (b10,), emit_to(oa_ref))
    )
    pl.when(jnp.logical_not(a_here))(lambda: empty(oa_ref))
    pl.when(b_here)(lambda: attend(qb_ref, (k_ref,), (v_ref,), (b02,), emit_to(ob_ref)))
    pl.when(jnp.logical_not(b_here))(lambda: empty(ob_ref))


def merge_kernel(rows, lens_ref, o_ref, lse_ref, ra_ref, rb_ref, all_ref, out_ref):
    span = lens_ref[lens_ref.shape[0] - 1]
    step = 128
    eye = lax.broadcasted_iota(jnp.int32, (128, 128), 0) == lax.broadcasted_iota(
        jnp.int32, (128, 128), 1
    )

    @pl.when(span < 2)
    def _():
        out_ref[...] = o_ref[...]

    @pl.when(span >= 2)
    def _():
        blocks = rows // step
        head_lane = lax.broadcasted_iota(jnp.int32, (step, 128), 1) == pl.program_id(0)
        stat_a = ra_ref[rows:, :].astype(jnp.float32)
        stat_b = rb_ref[rows:, :].astype(jnp.float32)

        def column(stats, i):
            row = (stats[i : i + 1] + stats[blocks + i : blocks + i + 1]) + stats[
                2 * blocks + i : 2 * blocks + i + 1
            ]
            return jnp.sum(jnp.where(eye, row, 0.0), axis=1, keepdims=True)

        for i in range(blocks):
            r = i * step
            own = jnp.sum(jnp.where(head_lane, lse_ref[r : r + step, :], 0.0), axis=1, keepdims=True)
            lse_a = column(stat_a, i)
            lse_b = jnp.where(span == 3, column(stat_b, i), NEG)
            top = jnp.maximum(own, jnp.maximum(lse_a, lse_b))
            w0 = jnp.exp2(own - top)
            w1 = jnp.exp2(lse_a - top)
            w2 = jnp.exp2(lse_b - top)
            total = (
                o_ref[r : r + step, :].astype(jnp.float32) * w0
                + ra_ref[r : r + step, :].astype(jnp.float32) * w1
                + rb_ref[r : r + step, :].astype(jnp.float32) * w2
            )
            out_ref[r : r + step, :] = (total / (w0 + w1 + w2)).astype(jnp.bfloat16)


def attention_fast(attn_query, attn_key, attn_value, lengths, hyena_out):
    rows, cols = attn_query.shape
    span_index = lax.axis_index("seq")
    scalars = jnp.concatenate((lengths, jnp.reshape(span_index, (1,)).astype(jnp.int32)))
    all_heads = cols // HD
    heads = all_heads * 3 // 8
    near = all_heads - 2 * heads
    width = heads * HD
    smem = pl.BlockSpec(memory_space=pltpu.SMEM)
    block = pl.BlockSpec((rows, HD), lambda h: (0, h))
    tall = pl.BlockSpec((rows + STAT_ROWS, HD), lambda h: (0, h))
    packed = pl.BlockSpec((rows, 128), lambda h: (0, 0))

    def at(offset):
        return pl.BlockSpec((rows, HD), lambda h: (0, offset + h))

    def pair(lo, hi):
        return jnp.concatenate((attn_key[:, lo:hi], attn_value[:, lo:hi]), axis=1)

    sent = []
    for c in range(2):
        qc = attn_query[:, c * width : (c + 1) * width]
        qa = lax.ppermute(qc, "seq", [(2, 1), (3, 2)])
        qb = lax.ppermute(qc, "seq", [(3, 1)])
        kv = pair(c * width, (c + 1) * width)
        sent.append((qa, qb, lax.ppermute(kv, "seq", [(0, 1)])))
    kv = pair(2 * width, cols)
    kv1 = lax.ppermute(kv, "seq", [(0, 1), (1, 2), (2, 3)])
    kv2 = lax.ppermute(kv, "seq", [(0, 2), (1, 3)])
    scalars, hyena_out = lax.optimization_barrier((scalars, hyena_out))
    outs = []
    for c in range(2):
        qa, qb, kvp = sent[c]
        whole = at(c * heads)
        own, lse, oa, ob = pl.pallas_call(
            lambda *refs: attn_kernel(rows, *refs),
            grid=(heads,),
            out_shape=(
                jax.ShapeDtypeStruct((rows, width), jnp.bfloat16),
                jax.ShapeDtypeStruct((rows, 128), jnp.float32),
                jax.ShapeDtypeStruct((rows + STAT_ROWS, width), jnp.bfloat16),
                jax.ShapeDtypeStruct((rows + STAT_ROWS, width), jnp.bfloat16),
            ),
            in_specs=[smem, whole, block, block, block, at(heads), whole, whole],
            out_specs=(block, packed, tall, tall),
            scratch_shapes=[pltpu.VMEM((rows, rows), jnp.float32)] * 5,
            compiler_params=pltpu.CompilerParams(vmem_limit_bytes=32 * 2**20),
            cost_estimate=pl.CostEstimate(
                flops=heads * 5 * rows * rows * HD * 4 * 2,
                bytes_accessed=8 * 2**20,
                transcendentals=heads * 5 * rows * rows,
            ),
            name="attend",
        )(scalars, attn_query, qa, qb, kvp, kvp, attn_key, attn_value)
        ra = lax.ppermute(oa, "seq", [(1, 2), (2, 3)])
        rb = lax.ppermute(ob, "seq", [(1, 3)])
        outs.append((own, lse, ra, rb))
        scalars, _ = lax.optimization_barrier((scalars, own))
    anywhere = pl.BlockSpec(memory_space=pl.ANY)
    whole_out = jax.ShapeDtypeStruct((rows, cols), jnp.bfloat16)
    mine = at(2 * heads)
    result = pl.pallas_call(
        lambda *refs: near_kernel(rows, *refs[:8], None, *refs[8:]),
        grid=(near,),
        out_shape=whole_out,
        in_specs=[smem, mine, mine, mine, block, at(near), block, at(near)],
        out_specs=mine,
        scratch_shapes=[pltpu.VMEM((rows, rows), jnp.float32)] * 3,
        compiler_params=pltpu.CompilerParams(vmem_limit_bytes=32 * 2**20),
        cost_estimate=pl.CostEstimate(
            flops=near * 3 * rows * rows * HD * 4 * 2,
            bytes_accessed=4 * 2**20,
            transcendentals=near * 3 * rows * rows,
        ),
        name="near",
    )(scalars, attn_query, attn_key, attn_value, kv1, kv1, kv2, kv2)
    for c in range(2):
        own, lse, ra, rb = outs[c]
        result = pl.pallas_call(
            lambda *refs: merge_kernel(rows, *refs),
            grid=(heads,),
            out_shape=whole_out,
            in_specs=[smem, block, packed, tall, tall, anywhere],
            out_specs=at(c * heads),
            input_output_aliases={5: 0},
            cost_estimate=pl.CostEstimate(
                flops=rows * width * 16, bytes_accessed=4 * 2**20, transcendentals=0
            ),
            name="merge",
        )(scalars, own, lse, ra, rb, result)
    return hyena_out, result


def local(
    features, short_filter, medium_filter, skip_gain, attn_query, attn_key, attn_value, lengths
):
    rows, cols = attn_query.shape
    spans = lax.axis_size("seq")
    taps = medium_filter.shape[0]
    if cols % 128 == 0 and taps % 128 == 0 and rows % taps == 0:
        hyena = hyena_fast
    else:
        hyena = hyena_mix
    hyena_out = hyena(features, short_filter, medium_filter, skip_gain, lengths)
    if spans == 4 and rows % 128 == 0 and rows <= 640 and cols % (8 * HD) == 0:
        return attention_fast(attn_query, attn_key, attn_value, lengths, hyena_out)
    return (hyena_out, attention_mix(attn_query, attn_key, attn_value, lengths))


def solution(mesh):
    in_specs = (
        P(("groups", "seq"), None, ("tensor", "sub")),
        P(None, ("tensor", "sub")),
        P(None, ("tensor", "sub")),
        P(("tensor", "sub")),
        P(("groups", "seq"), ("tensor", "sub")),
        P(("groups", "seq"), ("tensor", "sub")),
        P(("groups", "seq"), ("tensor", "sub")),
        P("groups"),
    )
    out_specs = (P(("groups", "seq"), ("tensor", "sub")), P(("groups", "seq"), ("tensor", "sub")))
    return jax.shard_map(local, mesh=mesh, in_specs=in_specs, out_specs=out_specs, check_vma=False)
```

```python
import math

import jax
import jax.numpy as jnp
import numpy as np
from jax import lax
from jax.experimental import pallas as pl
from jax.experimental.pallas import tpu as pltpu
from jax.sharding import PartitionSpec as P

HD = 128


def passed_along(value, axis, by):
    length = lax.axis_size(axis)
    pairs = [(i, i + by) for i in range(length) if 0 <= i + by < length]
    return lax.ppermute(value, axis, pairs)


def doc_of(positions, lengths):
    doc_ends = jnp.cumsum(lengths, dtype=jnp.int32)
    return jnp.sum(
        (positions[:, None] >= doc_ends[None, :]).astype(jnp.int32), axis=1, dtype=jnp.int32
    )


def hyena_mix(features, short_filter, medium_filter, skip_gain, lengths):
    row_count = features.shape[0]
    medium_taps = medium_filter.shape[0]
    rim_rows = medium_taps - 1
    span_index = lax.axis_index("seq")
    queries = features[:, 0].astype(jnp.float32)
    gated = (features[:, 1].astype(jnp.float32) * features[:, 2].astype(jnp.float32)).astype(
        jnp.bfloat16
    )
    gated = lax.optimization_barrier(gated)
    carried = passed_along(gated[row_count - rim_rows :], "seq", 1)
    extended = jnp.concatenate((carried, gated), axis=0)
    ext_positions = (
        span_index * row_count - rim_rows + jnp.arange(row_count + rim_rows, dtype=jnp.int32)
    )
    ext_docs = doc_of(ext_positions, lengths)
    ext_live = ext_positions >= 0
    own_docs = ext_docs[rim_rows:]

    def tap_term(tap_index, filter_bank):
        first_row = rim_rows - tap_index
        window = lax.dynamic_slice_in_dim(extended, first_row, row_count, 0).astype(jnp.float32)
        same_doc = lax.dynamic_slice_in_dim(ext_docs, first_row, row_count, 0) == own_docs
        live_mask = lax.dynamic_slice_in_dim(ext_live, first_row, row_count, 0)
        keep_mask = (same_doc & live_mask).astype(jnp.float32)[:, None]
        taps = lax.dynamic_index_in_dim(filter_bank, tap_index, 0, keepdims=False)
        return taps[None, :] * window * keep_mask

    short_sum = jnp.zeros(gated.shape, jnp.float32)
    for tap_index in range(short_filter.shape[0]):
        short_sum = short_sum + tap_term(tap_index, short_filter)

    def tap_block(block_index, partial_value):
        for offset in range(8):
            partial_value = partial_value + tap_term(block_index * 8 + offset, medium_filter)
        return partial_value

    medium_sum = lax.fori_loop(0, medium_taps // 8, tap_block, jnp.zeros(gated.shape, jnp.float32))
    mixed = queries * (short_sum + medium_sum + skip_gain[None, :] * gated.astype(jnp.float32))
    return mixed.astype(jnp.bfloat16)


def attention_mix(attn_query, attn_key, attn_value, lengths):
    row_count, col_count = attn_query.shape
    heads_here = col_count // HD
    span_index = lax.axis_index("seq")
    query_positions = span_index * row_count + jnp.arange(row_count, dtype=jnp.int32)
    query_docs = doc_of(query_positions, lengths)
    query_heads = attn_query.reshape(row_count, heads_here, HD)
    score_scale = HD ** (-0.5)
    last_query = query_positions[row_count - 1]
    first_query_doc = query_docs[0]

    def absorb(state_now, key_block, value_block, first_row):
        key_count = key_block.shape[0]
        last_key = first_row + key_count - 1
        last_key_doc = doc_of(jnp.reshape(last_key, (1,)), lengths)[0]
        masked_out = (first_row > last_query) | (last_key < 0) | (last_key_doc < first_query_doc)

        def compute(state_in):
            running_max, running_total, running_sum = state_in
            key_heads = key_block.reshape(key_count, heads_here, HD)
            value_heads = value_block.reshape(key_count, heads_here, HD)
            scores = (
                jnp.einsum(
                    "rhd,nhd->hrn", query_heads, key_heads, preferred_element_type=jnp.float32
                )
                * score_scale
            )
            key_positions = first_row + jnp.arange(key_count, dtype=jnp.int32)
            key_docs = doc_of(key_positions, lengths)
            allowed = (
                (key_positions[None, :] <= query_positions[:, None])
                & (key_docs[None, :] == query_docs[:, None])
                & (key_positions >= 0)[None, :]
            )
            masked = jnp.where(allowed[None], scores, -1e30)
            new_max = jnp.maximum(running_max, jnp.max(masked, axis=2))
            rescale = jnp.exp(running_max - new_max)
            weights = jnp.where(allowed[None], jnp.exp(scores - new_max[:, :, None]), 0.0)
            new_total = running_total * rescale + jnp.sum(weights, axis=2)
            product = jnp.einsum(
                "hrn,nhd->hrd",
                weights.astype(jnp.bfloat16),
                value_heads,
                preferred_element_type=jnp.float32,
            )
            new_sum = running_sum * rescale[:, :, None] + product
            return (new_max, new_total, new_sum)

        def keep_state(state_in):
            return state_in

        return lax.cond(masked_out, keep_state, compute, state_now)

    def fold_keys(state_now, pieces, first_row):
        key_all, value_all = pieces
        key_count = key_all.shape[0]
        block_rows = math.gcd(key_count, 1536)
        if block_rows == key_count:
            return absorb(state_now, key_all, value_all, first_row)
        block_total = key_count // block_rows
        key_blocks = key_all.reshape(block_total, block_rows, col_count)
        value_blocks = value_all.reshape(block_total, block_rows, col_count)

        def scan_step(state_inner, block_items):
            key_block, value_block, block_index = block_items
            return (
                absorb(state_inner, key_block, value_block, first_row + block_index * block_rows),
                None,
            )

        state_now, unused = lax.scan(
            scan_step,
            state_now,
            (key_blocks, value_blocks, jnp.arange(block_total, dtype=jnp.int32)),
        )
        return state_now

    initial = (
        jnp.full((heads_here, row_count), -1e30, jnp.float32),
        jnp.zeros((heads_here, row_count), jnp.float32),
        jnp.zeros((heads_here, row_count, HD), jnp.float32),
    )
    state_now = fold_keys(
        initial,
        (
            lax.all_gather(attn_key, "seq", axis=0, tiled=True),
            lax.all_gather(attn_value, "seq", axis=0, tiled=True),
        ),
        jnp.int32(0),
    )
    running_max, running_total, running_sum = state_now
    result = running_sum / running_total[:, :, None]
    return result.transpose(1, 0, 2).reshape(row_count, col_count).astype(jnp.bfloat16)


LOG2E = 1.4426950408889634
LN2 = 0.6931471805599453
SCALE2 = HD**-0.5 * LOG2E
NEG = -1e30
STAT_ROWS = 16


def hyena_kernel(row_count, taps, lens_ref, feat_ref, rim_ref, filt_ref, fwd_ref, inv_ref, out_ref,
                 ext_ref, sum_ref):
    base = lens_ref[lens_ref.shape[0] - 1]
    ext_ref[:taps, :] = rim_ref[...]
    ext_ref[taps:, :] = (
        feat_ref[1].astype(jnp.float32) * feat_ref[2].astype(jnp.float32)
    ).astype(jnp.bfloat16)

    def dot(x, y):
        return jnp.dot(x, y, preferred_element_type=jnp.float32)

    filt = filt_ref[...]
    filt_hi = filt.astype(jnp.bfloat16)
    filt_lo = (filt - filt_hi.astype(jnp.float32)).astype(jnp.bfloat16)
    spec = (
        dot(fwd_ref[0, :, :taps], filt_hi)
        + dot(fwd_ref[1, :, :taps], filt_hi)
        + dot(fwd_ref[0, :, :taps], filt_lo)
    )
    spec_r, spec_i = spec[:taps], spec[taps:]
    win_iota = lax.broadcasted_iota(jnp.int32, (2 * taps, 1), 0)
    out_iota = lax.broadcasted_iota(jnp.int32, (taps, 1), 0)
    for block in range(row_count // taps):
        r0 = block * taps
        start = jnp.int32(0)
        for doc in range(lens_ref.shape[0] - 1):
            end = start + lens_ref[doc]
            first, last = start - base, end - base

            @pl.when((last > r0) & (first < r0 + taps) & (first < last))
            def _(first=first):
                window = ext_ref[r0 : r0 + 2 * taps, :]
                window = jnp.where(win_iota + (r0 - taps) >= first, window, jnp.zeros_like(window))
                wave = dot(fwd_ref[0], window) + dot(fwd_ref[1], window)
                wave_r, wave_i = wave[:taps], wave[taps:]
                prod = jnp.concatenate(
                    (
                        (wave_r * spec_r - wave_i * spec_i).astype(jnp.bfloat16),
                        (wave_r * spec_i + wave_i * spec_r).astype(jnp.bfloat16),
                    ),
                    axis=0,
                )
                sums = dot(inv_ref[0], prod) + dot(inv_ref[1], prod)
                sum_ref[...] = jnp.where(out_iota + r0 >= first, sums, sum_ref[...])

            start = end
        out_ref[r0 : r0 + taps, :] = (
            feat_ref[0, r0 : r0 + taps, :].astype(jnp.float32) * sum_ref[...]
        ).astype(out_ref.dtype)


def split_two(matrix):
    high = matrix.astype(jnp.bfloat16)
    low = (matrix - high.astype(np.float64)).astype(jnp.bfloat16)
    return np.stack((high, low))


def hyena_fast(features, short_filter, medium_filter, skip_gain, lengths):
    row_count, _, cols = features.shape
    taps = medium_filter.shape[0]
    span_index = lax.axis_index("seq")
    streams = features.transpose(1, 0, 2)
    tail = streams[:, row_count - taps :]
    gated_tail = (tail[1].astype(jnp.float32) * tail[2].astype(jnp.float32)).astype(jnp.bfloat16)
    carried = passed_along(gated_tail, "seq", 1)
    head = jnp.concatenate((short_filter[:1] + skip_gain[None, :], short_filter[1:]), axis=0)
    filt = medium_filter + jnp.pad(head, ((0, taps - head.shape[0]), (0, 0)))
    angle = np.pi / (2 * taps) * np.outer(2 * np.arange(taps) + 1, np.arange(2 * taps))
    fwd = split_two(np.concatenate((np.cos(angle), -np.sin(angle)), axis=0))
    inv = split_two(
        np.concatenate((np.cos(angle), -np.sin(angle)), axis=0).T[taps:] / taps
    )
    scalars = jnp.concatenate((lengths, jnp.reshape(span_index * row_count, (1,)).astype(jnp.int32)))
    width = math.gcd(cols, 512)
    return pl.pallas_call(
        lambda *refs: hyena_kernel(row_count, taps, *refs),
        grid=(cols // width,),
        out_shape=jax.ShapeDtypeStruct((row_count, cols), jnp.bfloat16),
        in_specs=[
            pl.BlockSpec(memory_space=pltpu.SMEM),
            pl.BlockSpec((3, row_count, width), lambda i: (0, 0, i)),
            pl.BlockSpec((taps, width), lambda i: (0, i)),
            pl.BlockSpec((taps, width), lambda i: (0, i)),
            pl.BlockSpec(fwd.shape, lambda i: (0, 0, 0)),
            pl.BlockSpec(inv.shape, lambda i: (0, 0, 0)),
        ],
        out_specs=pl.BlockSpec((row_count, width), lambda i: (0, i)),
        scratch_shapes=[
            pltpu.VMEM((row_count + taps, width), jnp.bfloat16),
            pltpu.VMEM((taps, width), jnp.float32),
        ],
        compiler_params=pltpu.CompilerParams(vmem_limit_bytes=32 * 2**20),
        cost_estimate=pl.CostEstimate(
            flops=2 * 9 * 2 * taps * taps * 3 * cols, bytes_accessed=8 * 2**20, transcendentals=0
        ),
        name="hyena",
    )(scalars, streams, carried, filt, fwd, inv)


def doc_start(pos, lens_ref):
    start = jnp.zeros_like(pos)
    end = jnp.int32(0)
    for doc in range(lens_ref.shape[0] - 1):
        end = end + lens_ref[doc]
        start = jnp.where(pos >= end, end, start)
    return start


def attend(query_ref, keys, values, biases, backs, emit):
    rows = query_ref.shape[0]
    step = 128
    ones = jnp.ones((rows, 128), jnp.bfloat16)
    vals = [jnp.concatenate((v[...], ones), axis=1) for v in values]
    for r in range(0, rows, step):
        q = query_ref[r : r + step, :]
        cuts = [(0, r + step) if back == 0 else (r, rows) if back == 2 else (0, rows) for back in backs]
        scores = [
            lax.dot_general(q, k[lo:hi, :], (((1,), (1,)), ((), ())),
                            preferred_element_type=jnp.float32) + b[r : r + step, lo:hi]
            for k, b, (lo, hi) in zip(keys, biases, cuts)
        ]
        top = jnp.max(scores[0], axis=1, keepdims=True)
        for s in scores[1:]:
            top = jnp.maximum(top, jnp.max(s, axis=1, keepdims=True))
        acc = None
        for s, v, (lo, hi) in zip(scores, vals, cuts):
            w = jnp.exp2((s - top) * SCALE2).astype(jnp.bfloat16)
            part = jnp.dot(w, v[lo:hi], preferred_element_type=jnp.float32)
            acc = part if acc is None else acc + part
        total = acc[:, 128:]
        emit(r, acc[:, :128] / total, top * SCALE2 + jnp.log2(total))


def needs(lens_ref, base, rows, ahead, back):
    q_first = base + ahead * rows
    start = jnp.int32(0)
    end = jnp.int32(0)
    for doc in range(lens_ref.shape[0] - 1):
        end = end + lens_ref[doc]
        start = jnp.where(q_first >= end, end, start)
    return start < base + (1 - back) * rows


def fill_bias(lens_ref, base, rows, ref, ahead, back):
    qpos = base + ahead * rows + lax.broadcasted_iota(jnp.int32, (rows, 1), 0)
    starts = doc_start(qpos, lens_ref)
    kpos = base - back * rows + lax.broadcasted_iota(jnp.int32, (1, rows), 1)
    ref[...] = jnp.where((kpos <= qpos) & (kpos >= starts), 0.0, NEG).astype(jnp.float32)


def near_kernel(rows, lens_ref, q_ref, k_ref, v_ref, k1_ref, v1_ref, k2_ref, v2_ref, all_ref, o_ref,
                b0, b1, b2):
    span = lens_ref[lens_ref.shape[0] - 1]
    base = span * rows
    one = (span >= 1) & needs(lens_ref, base, rows, 0, 1)
    two = (span >= 2) & needs(lens_ref, base, rows, 0, 2)

    @pl.when(pl.program_id(0) == 0)
    def _():
        fill_bias(lens_ref, base, rows, b0, 0, 0)
        pl.when(one)(lambda: fill_bias(lens_ref, base, rows, b1, 0, 1))
        pl.when(two)(lambda: fill_bias(lens_ref, base, rows, b2, 0, 2))

    def emit(r, out, lse):
        o_ref[r : r + 128, :] = out.astype(jnp.bfloat16)

    pl.when(two)(
        lambda: attend(q_ref, (k_ref, k1_ref, k2_ref), (v_ref, v1_ref, v2_ref), (b0, b1, b2), (0, 1, 2), emit)
    )
    pl.when(one & jnp.logical_not(two))(
        lambda: attend(q_ref, (k_ref, k1_ref), (v_ref, v1_ref), (b0, b1), (0, 1), emit)
    )
    pl.when(jnp.logical_not(one))(lambda: attend(q_ref, (k_ref,), (v_ref,), (b0,), (0,), emit))


def attn_kernel(rows, lens_ref, q_ref, qa_ref, qb_ref, kp_ref, vp_ref, k_ref, v_ref,
                o_ref, lse_ref, oa_ref, ob_ref, b00, b10, b01, b11, b02):
    span = lens_ref[lens_ref.shape[0] - 1]
    base = span * rows

    def reads(ahead, back):
        return needs(lens_ref, base, rows, ahead, back)

    own_prev = (span == 1) & reads(0, 1)
    a_here = ((span == 1) | (span == 2)) & reads(1, 0)
    a_prev = (span == 1) & reads(1, 1)
    b_here = (span == 1) & reads(2, 0)

    @pl.when(pl.program_id(0) == 0)
    def _():
        lse_ref[...] = jnp.zeros_like(lse_ref)

        def fill(ref, ahead, back):
            fill_bias(lens_ref, base, rows, ref, ahead, back)

        fill(b00, 0, 0)
        pl.when(own_prev)(lambda: fill(b01, 0, 1))
        pl.when(a_here)(lambda: fill(b10, 1, 0))
        pl.when(a_prev)(lambda: fill(b11, 1, 1))
        pl.when(b_here)(lambda: fill(b02, 2, 0))

    step = 128
    head_lane = lax.broadcasted_iota(jnp.int32, (step, 128), 1) == pl.program_id(0)

    def emit_own(r, out, lse):
        o_ref[r : r + step, :] = out.astype(jnp.bfloat16)
        lse_ref[r : r + step, :] = jnp.where(head_lane, lse, lse_ref[r : r + step, :])

    eye = lax.broadcasted_iota(jnp.int32, (128, 128), 0) == lax.broadcasted_iota(
        jnp.int32, (128, 128), 1
    )
    stat_iota = lax.broadcasted_iota(jnp.int32, (STAT_ROWS, 128), 0)

    def emit_to(ref):
        stats = [jnp.zeros((STAT_ROWS, 128), jnp.float32)]

        def emit(r, out, lse):
            ref[r : r + step, :] = out.astype(jnp.bfloat16)
            rest = jnp.sum(jnp.where(eye, lse, 0.0), axis=0, keepdims=True)
            for piece in range(3):
                high = rest.astype(jnp.bfloat16).astype(jnp.float32)
                stats[0] = jnp.where(stat_iota == piece * (rows // step) + r // step, high, stats[0])
                rest = rest - high
            if r + step == rows:
                ref[rows:, :] = stats[0].astype(jnp.bfloat16)

        return emit

    def empty(ref):
        ref[:rows, :] = jnp.zeros((rows, 128), jnp.bfloat16)
        ref[rows:, :] = jnp.where(stat_iota < rows // step, NEG, 0.0).astype(jnp.bfloat16)

    pl.when(own_prev)(lambda: attend(q_ref, (kp_ref, k_ref), (vp_ref, v_ref), (b01, b00), (1, 0), emit_own))
    pl.when(jnp.logical_not(own_prev))(lambda: attend(q_ref, (k_ref,), (v_ref,), (b00,), (0,), emit_own))
    pl.when(a_prev)(
        lambda: attend(qa_ref, (kp_ref, k_ref), (vp_ref, v_ref), (b11, b10), (2, 1), emit_to(oa_ref))
    )
    pl.when(a_here & jnp.logical_not(a_prev))(
        lambda: attend(qa_ref, (k_ref,), (v_ref,), (b10,), (1,), emit_to(oa_ref))
    )
    pl.when(jnp.logical_not(a_here))(lambda: empty(oa_ref))
    pl.when(b_here)(lambda: attend(qb_ref, (k_ref,), (v_ref,), (b02,), (2,), emit_to(ob_ref)))
    pl.when(jnp.logical_not(b_here))(lambda: empty(ob_ref))


def merge_kernel(rows, lens_ref, o_ref, lse_ref, ra_ref, rb_ref, all_ref, out_ref):
    span = lens_ref[lens_ref.shape[0] - 1]
    step = 128
    eye = lax.broadcasted_iota(jnp.int32, (128, 128), 0) == lax.broadcasted_iota(
        jnp.int32, (128, 128), 1
    )

    @pl.when(span < 2)
    def _():
        out_ref[...] = o_ref[...]

    @pl.when(span >= 2)
    def _():
        blocks = rows // step
        head_lane = lax.broadcasted_iota(jnp.int32, (step, 128), 1) == pl.program_id(0)
        stat_a = ra_ref[rows:, :].astype(jnp.float32)
        stat_b = rb_ref[rows:, :].astype(jnp.float32)

        def column(stats, i):
            row = (stats[i : i + 1] + stats[blocks + i : blocks + i + 1]) + stats[
                2 * blocks + i : 2 * blocks + i + 1
            ]
            return jnp.sum(jnp.where(eye, row, 0.0), axis=1, keepdims=True)

        for i in range(blocks):
            r = i * step
            own = jnp.sum(jnp.where(head_lane, lse_ref[r : r + step, :], 0.0), axis=1, keepdims=True)
            lse_a = column(stat_a, i)
            lse_b = jnp.where(span == 3, column(stat_b, i), NEG)
            top = jnp.maximum(own, jnp.maximum(lse_a, lse_b))
            w0 = jnp.exp2(own - top)
            w1 = jnp.exp2(lse_a - top)
            w2 = jnp.exp2(lse_b - top)
            total = (
                o_ref[r : r + step, :].astype(jnp.float32) * w0
                + ra_ref[r : r + step, :].astype(jnp.float32) * w1
                + rb_ref[r : r + step, :].astype(jnp.float32) * w2
            )
            out_ref[r : r + step, :] = (total / (w0 + w1 + w2)).astype(jnp.bfloat16)


def attention_fast(attn_query, attn_key, attn_value, lengths, hyena_out):
    rows, cols = attn_query.shape
    span_index = lax.axis_index("seq")
    scalars = jnp.concatenate((lengths, jnp.reshape(span_index, (1,)).astype(jnp.int32)))
    all_heads = cols // HD
    heads = all_heads * 3 // 8
    near = all_heads - 2 * heads
    width = heads * HD
    smem = pl.BlockSpec(memory_space=pltpu.SMEM)
    block = pl.BlockSpec((rows, HD), lambda h: (0, h))
    tall = pl.BlockSpec((rows + STAT_ROWS, HD), lambda h: (0, h))
    packed = pl.BlockSpec((rows, 128), lambda h: (0, 0))

    def at(offset):
        return pl.BlockSpec((rows, HD), lambda h: (0, offset + h))

    def pair(lo, hi):
        return jnp.concatenate((attn_key[:, lo:hi], attn_value[:, lo:hi]), axis=1)

    sent = []
    for c in range(2):
        qc = attn_query[:, c * width : (c + 1) * width]
        qa = lax.ppermute(qc, "seq", [(2, 1), (3, 2)])
        qb = lax.ppermute(qc, "seq", [(3, 1)])
        kv = pair(c * width, (c + 1) * width)
        sent.append((qa, qb, lax.ppermute(kv, "seq", [(0, 1)])))
    kv = pair(2 * width, cols)
    kv1 = lax.ppermute(kv, "seq", [(0, 1), (1, 2), (2, 3)])
    kv2 = lax.ppermute(kv1, "seq", [(1, 2), (2, 3)])
    scalars, hyena_out, kv1, kv2 = lax.optimization_barrier((scalars, hyena_out, kv1, kv2))
    outs = []
    for c in range(2):
        qa, qb, kvp = sent[c]
        whole = at(c * heads)
        own, lse, oa, ob = pl.pallas_call(
            lambda *refs: attn_kernel(rows, *refs),
            grid=(heads,),
            out_shape=(
                jax.ShapeDtypeStruct((rows, width), jnp.bfloat16),
                jax.ShapeDtypeStruct((rows, 128), jnp.float32),
                jax.ShapeDtypeStruct((rows + STAT_ROWS, width), jnp.bfloat16),
                jax.ShapeDtypeStruct((rows + STAT_ROWS, width), jnp.bfloat16),
            ),
            in_specs=[smem, whole, block, block, block, at(heads), whole, whole],
            out_specs=(block, packed, tall, tall),
            scratch_shapes=[pltpu.VMEM((rows, rows), jnp.float32)] * 5,
            compiler_params=pltpu.CompilerParams(vmem_limit_bytes=32 * 2**20),
            cost_estimate=pl.CostEstimate(
                flops=heads * 5 * rows * rows * HD * 4 * 2,
                bytes_accessed=8 * 2**20,
                transcendentals=heads * 5 * rows * rows,
            ),
            name="attend",
        )(scalars, attn_query, qa, qb, kvp, kvp, attn_key, attn_value)
        ra = lax.ppermute(oa, "seq", [(1, 2), (2, 3)])
        rb = lax.ppermute(ob, "seq", [(1, 3)])
        outs.append((own, lse, ra, rb))
        scalars, _ = lax.optimization_barrier((scalars, own))
    anywhere = pl.BlockSpec(memory_space=pl.ANY)
    whole_out = jax.ShapeDtypeStruct((rows, cols), jnp.bfloat16)
    mine = at(2 * heads)
    result = pl.pallas_call(
        lambda *refs: near_kernel(rows, *refs[:8], None, *refs[8:]),
        grid=(near,),
        out_shape=whole_out,
        in_specs=[smem, mine, mine, mine, block, at(near), block, at(near)],
        out_specs=mine,
        scratch_shapes=[pltpu.VMEM((rows, rows), jnp.float32)] * 3,
        compiler_params=pltpu.CompilerParams(vmem_limit_bytes=32 * 2**20),
        cost_estimate=pl.CostEstimate(
            flops=near * 3 * rows * rows * HD * 4 * 2,
            bytes_accessed=4 * 2**20,
            transcendentals=near * 3 * rows * rows,
        ),
        name="near",
    )(scalars, attn_query, attn_key, attn_value, kv1, kv1, kv2, kv2)
    for c in range(2):
        own, lse, ra, rb = outs[c]
        result = pl.pallas_call(
            lambda *refs: merge_kernel(rows, *refs),
            grid=(heads,),
            out_shape=whole_out,
            in_specs=[smem, block, packed, tall, tall, anywhere],
            out_specs=at(c * heads),
            input_output_aliases={5: 0},
            cost_estimate=pl.CostEstimate(
                flops=rows * width * 16, bytes_accessed=4 * 2**20, transcendentals=0
            ),
            name="merge",
        )(scalars, own, lse, ra, rb, result)
    return hyena_out, result


def local(
    features, short_filter, medium_filter, skip_gain, attn_query, attn_key, attn_value, lengths
):
    rows, cols = attn_query.shape
    spans = lax.axis_size("seq")
    taps = medium_filter.shape[0]
    if cols % 128 == 0 and taps % 128 == 0 and rows % taps == 0:
        hyena = hyena_fast
    else:
        hyena = hyena_mix
    hyena_out = hyena(features, short_filter, medium_filter, skip_gain, lengths)
    if spans == 4 and rows % 128 == 0 and rows <= 640 and cols % (8 * HD) == 0:
        return attention_fast(attn_query, attn_key, attn_value, lengths, hyena_out)
    return (hyena_out, attention_mix(attn_query, attn_key, attn_value, lengths))


def solution(mesh):
    in_specs = (
        P(("groups", "seq"), None, ("tensor", "sub")),
        P(None, ("tensor", "sub")),
        P(None, ("tensor", "sub")),
        P(("tensor", "sub")),
        P(("groups", "seq"), ("tensor", "sub")),
        P(("groups", "seq"), ("tensor", "sub")),
        P(("groups", "seq"), ("tensor", "sub")),
        P("groups"),
    )
    out_specs = (P(("groups", "seq"), ("tensor", "sub")), P(("groups", "seq"), ("tensor", "sub")))
    return jax.shard_map(local, mesh=mesh, in_specs=in_specs, out_specs=out_specs, check_vma=False)
```

```python
import math

import jax
import jax.numpy as jnp
import numpy as np
from jax import lax
from jax.experimental import pallas as pl
from jax.experimental.pallas import tpu as pltpu
from jax.sharding import PartitionSpec as P

HD = 128


def passed_along(value, axis, by):
    length = lax.axis_size(axis)
    pairs = [(i, i + by) for i in range(length) if 0 <= i + by < length]
    return lax.ppermute(value, axis, pairs)


def doc_of(positions, lengths):
    doc_ends = jnp.cumsum(lengths, dtype=jnp.int32)
    return jnp.sum(
        (positions[:, None] >= doc_ends[None, :]).astype(jnp.int32), axis=1, dtype=jnp.int32
    )


def hyena_mix(features, short_filter, medium_filter, skip_gain, lengths):
    row_count = features.shape[0]
    medium_taps = medium_filter.shape[0]
    rim_rows = medium_taps - 1
    span_index = lax.axis_index("seq")
    queries = features[:, 0].astype(jnp.float32)
    gated = (features[:, 1].astype(jnp.float32) * features[:, 2].astype(jnp.float32)).astype(
        jnp.bfloat16
    )
    gated = lax.optimization_barrier(gated)
    carried = passed_along(gated[row_count - rim_rows :], "seq", 1)
    extended = jnp.concatenate((carried, gated), axis=0)
    ext_positions = (
        span_index * row_count - rim_rows + jnp.arange(row_count + rim_rows, dtype=jnp.int32)
    )
    ext_docs = doc_of(ext_positions, lengths)
    ext_live = ext_positions >= 0
    own_docs = ext_docs[rim_rows:]

    def tap_term(tap_index, filter_bank):
        first_row = rim_rows - tap_index
        window = lax.dynamic_slice_in_dim(extended, first_row, row_count, 0).astype(jnp.float32)
        same_doc = lax.dynamic_slice_in_dim(ext_docs, first_row, row_count, 0) == own_docs
        live_mask = lax.dynamic_slice_in_dim(ext_live, first_row, row_count, 0)
        keep_mask = (same_doc & live_mask).astype(jnp.float32)[:, None]
        taps = lax.dynamic_index_in_dim(filter_bank, tap_index, 0, keepdims=False)
        return taps[None, :] * window * keep_mask

    short_sum = jnp.zeros(gated.shape, jnp.float32)
    for tap_index in range(short_filter.shape[0]):
        short_sum = short_sum + tap_term(tap_index, short_filter)

    def tap_block(block_index, partial_value):
        for offset in range(8):
            partial_value = partial_value + tap_term(block_index * 8 + offset, medium_filter)
        return partial_value

    medium_sum = lax.fori_loop(0, medium_taps // 8, tap_block, jnp.zeros(gated.shape, jnp.float32))
    mixed = queries * (short_sum + medium_sum + skip_gain[None, :] * gated.astype(jnp.float32))
    return mixed.astype(jnp.bfloat16)


def attention_mix(attn_query, attn_key, attn_value, lengths):
    row_count, col_count = attn_query.shape
    heads_here = col_count // HD
    span_index = lax.axis_index("seq")
    query_positions = span_index * row_count + jnp.arange(row_count, dtype=jnp.int32)
    query_docs = doc_of(query_positions, lengths)
    query_heads = attn_query.reshape(row_count, heads_here, HD)
    score_scale = HD ** (-0.5)
    last_query = query_positions[row_count - 1]
    first_query_doc = query_docs[0]

    def absorb(state_now, key_block, value_block, first_row):
        key_count = key_block.shape[0]
        last_key = first_row + key_count - 1
        last_key_doc = doc_of(jnp.reshape(last_key, (1,)), lengths)[0]
        masked_out = (first_row > last_query) | (last_key < 0) | (last_key_doc < first_query_doc)

        def compute(state_in):
            running_max, running_total, running_sum = state_in
            key_heads = key_block.reshape(key_count, heads_here, HD)
            value_heads = value_block.reshape(key_count, heads_here, HD)
            scores = (
                jnp.einsum(
                    "rhd,nhd->hrn", query_heads, key_heads, preferred_element_type=jnp.float32
                )
                * score_scale
            )
            key_positions = first_row + jnp.arange(key_count, dtype=jnp.int32)
            key_docs = doc_of(key_positions, lengths)
            allowed = (
                (key_positions[None, :] <= query_positions[:, None])
                & (key_docs[None, :] == query_docs[:, None])
                & (key_positions >= 0)[None, :]
            )
            masked = jnp.where(allowed[None], scores, -1e30)
            new_max = jnp.maximum(running_max, jnp.max(masked, axis=2))
            rescale = jnp.exp(running_max - new_max)
            weights = jnp.where(allowed[None], jnp.exp(scores - new_max[:, :, None]), 0.0)
            new_total = running_total * rescale + jnp.sum(weights, axis=2)
            product = jnp.einsum(
                "hrn,nhd->hrd",
                weights.astype(jnp.bfloat16),
                value_heads,
                preferred_element_type=jnp.float32,
            )
            new_sum = running_sum * rescale[:, :, None] + product
            return (new_max, new_total, new_sum)

        def keep_state(state_in):
            return state_in

        return lax.cond(masked_out, keep_state, compute, state_now)

    def fold_keys(state_now, pieces, first_row):
        key_all, value_all = pieces
        key_count = key_all.shape[0]
        block_rows = math.gcd(key_count, 1536)
        if block_rows == key_count:
            return absorb(state_now, key_all, value_all, first_row)
        block_total = key_count // block_rows
        key_blocks = key_all.reshape(block_total, block_rows, col_count)
        value_blocks = value_all.reshape(block_total, block_rows, col_count)

        def scan_step(state_inner, block_items):
            key_block, value_block, block_index = block_items
            return (
                absorb(state_inner, key_block, value_block, first_row + block_index * block_rows),
                None,
            )

        state_now, unused = lax.scan(
            scan_step,
            state_now,
            (key_blocks, value_blocks, jnp.arange(block_total, dtype=jnp.int32)),
        )
        return state_now

    initial = (
        jnp.full((heads_here, row_count), -1e30, jnp.float32),
        jnp.zeros((heads_here, row_count), jnp.float32),
        jnp.zeros((heads_here, row_count, HD), jnp.float32),
    )
    state_now = fold_keys(
        initial,
        (
            lax.all_gather(attn_key, "seq", axis=0, tiled=True),
            lax.all_gather(attn_value, "seq", axis=0, tiled=True),
        ),
        jnp.int32(0),
    )
    running_max, running_total, running_sum = state_now
    result = running_sum / running_total[:, :, None]
    return result.transpose(1, 0, 2).reshape(row_count, col_count).astype(jnp.bfloat16)


LOG2E = 1.4426950408889634
LN2 = 0.6931471805599453
SCALE2 = HD**-0.5 * LOG2E
NEG = -1e30
STAT_ROWS = 16


def hyena_kernel(row_count, taps, lens_ref, feat_ref, rim_ref, filt_ref, fwd_ref, inv_ref, out_ref,
                 ext_ref, sum_ref):
    base = lens_ref[lens_ref.shape[0] - 1]
    ext_ref[:taps, :] = rim_ref[...]
    ext_ref[taps:, :] = (
        feat_ref[1].astype(jnp.float32) * feat_ref[2].astype(jnp.float32)
    ).astype(jnp.bfloat16)

    def dot(x, y):
        return jnp.dot(x, y, preferred_element_type=jnp.float32)

    filt = filt_ref[...]
    filt_hi = filt.astype(jnp.bfloat16)
    filt_lo = (filt - filt_hi.astype(jnp.float32)).astype(jnp.bfloat16)
    spec = (
        dot(fwd_ref[0, :, :taps], filt_hi)
        + dot(fwd_ref[1, :, :taps], filt_hi)
        + dot(fwd_ref[0, :, :taps], filt_lo)
    )
    spec_r, spec_i = spec[:taps], spec[taps:]
    win_iota = lax.broadcasted_iota(jnp.int32, (2 * taps, 1), 0)
    out_iota = lax.broadcasted_iota(jnp.int32, (taps, 1), 0)
    for block in range(row_count // taps):
        r0 = block * taps
        start = jnp.int32(0)
        for doc in range(lens_ref.shape[0] - 1):
            end = start + lens_ref[doc]
            first, last = start - base, end - base

            @pl.when((last > r0) & (first < r0 + taps) & (first < last))
            def _(first=first):
                window = ext_ref[r0 : r0 + 2 * taps, :]
                window = jnp.where(win_iota + (r0 - taps) >= first, window, jnp.zeros_like(window))
                wave = dot(fwd_ref[0], window) + dot(fwd_ref[1], window)
                wave_r, wave_i = wave[:taps], wave[taps:]
                prod = jnp.concatenate(
                    (
                        (wave_r * spec_r - wave_i * spec_i).astype(jnp.bfloat16),
                        (wave_r * spec_i + wave_i * spec_r).astype(jnp.bfloat16),
                    ),
                    axis=0,
                )
                sums = dot(inv_ref[0], prod) + dot(inv_ref[1], prod)
                sum_ref[...] = jnp.where(out_iota + r0 >= first, sums, sum_ref[...])

            start = end
        out_ref[r0 : r0 + taps, :] = (
            feat_ref[0, r0 : r0 + taps, :].astype(jnp.float32) * sum_ref[...]
        ).astype(out_ref.dtype)


def split_two(matrix):
    high = matrix.astype(jnp.bfloat16)
    low = (matrix - high.astype(np.float64)).astype(jnp.bfloat16)
    return np.stack((high, low))


def hyena_fast(features, short_filter, medium_filter, skip_gain, lengths):
    row_count, _, cols = features.shape
    taps = medium_filter.shape[0]
    span_index = lax.axis_index("seq")
    streams = features.transpose(1, 0, 2)
    tail = streams[:, row_count - taps :]
    gated_tail = (tail[1].astype(jnp.float32) * tail[2].astype(jnp.float32)).astype(jnp.bfloat16)
    carried = passed_along(gated_tail, "seq", 1)
    head = jnp.concatenate((short_filter[:1] + skip_gain[None, :], short_filter[1:]), axis=0)
    filt = medium_filter + jnp.pad(head, ((0, taps - head.shape[0]), (0, 0)))
    angle = np.pi / (2 * taps) * np.outer(2 * np.arange(taps) + 1, np.arange(2 * taps))
    fwd = split_two(np.concatenate((np.cos(angle), -np.sin(angle)), axis=0))
    inv = split_two(
        np.concatenate((np.cos(angle), -np.sin(angle)), axis=0).T[taps:] / taps
    )
    scalars = jnp.concatenate((lengths, jnp.reshape(span_index * row_count, (1,)).astype(jnp.int32)))
    width = math.gcd(cols, 512)
    return pl.pallas_call(
        lambda *refs: hyena_kernel(row_count, taps, *refs),
        grid=(cols // width,),
        out_shape=jax.ShapeDtypeStruct((row_count, cols), jnp.bfloat16),
        in_specs=[
            pl.BlockSpec(memory_space=pltpu.SMEM),
            pl.BlockSpec((3, row_count, width), lambda i: (0, 0, i)),
            pl.BlockSpec((taps, width), lambda i: (0, i)),
            pl.BlockSpec((taps, width), lambda i: (0, i)),
            pl.BlockSpec(fwd.shape, lambda i: (0, 0, 0)),
            pl.BlockSpec(inv.shape, lambda i: (0, 0, 0)),
        ],
        out_specs=pl.BlockSpec((row_count, width), lambda i: (0, i)),
        scratch_shapes=[
            pltpu.VMEM((row_count + taps, width), jnp.bfloat16),
            pltpu.VMEM((taps, width), jnp.float32),
        ],
        compiler_params=pltpu.CompilerParams(vmem_limit_bytes=32 * 2**20),
        cost_estimate=pl.CostEstimate(
            flops=2 * 9 * 2 * taps * taps * 3 * cols, bytes_accessed=8 * 2**20, transcendentals=0
        ),
        name="hyena",
    )(scalars, streams, carried, filt, fwd, inv)


def doc_start(pos, lens_ref):
    start = jnp.zeros_like(pos)
    end = jnp.int32(0)
    for doc in range(lens_ref.shape[0] - 1):
        end = end + lens_ref[doc]
        start = jnp.where(pos >= end, end, start)
    return start


def attend(query_ref, keys, values, biases, emit):
    rows = query_ref.shape[0]
    step = 128
    ones = jnp.ones((rows, 128), jnp.bfloat16)
    vals = [jnp.concatenate((v[...], ones), axis=1) for v in values]
    for r in range(0, rows, step):
        q = query_ref[r : r + step, :]
        scores = [
            lax.dot_general(q, k[...], (((1,), (1,)), ((), ())),
                            preferred_element_type=jnp.float32) + b[r : r + step, :]
            for k, b in zip(keys, biases)
        ]
        top = jnp.max(scores[0], axis=1, keepdims=True)
        for s in scores[1:]:
            top = jnp.maximum(top, jnp.max(s, axis=1, keepdims=True))
        acc = None
        for s, v in zip(scores, vals):
            w = jnp.exp2((s - top) * SCALE2).astype(jnp.bfloat16)
            part = jnp.dot(w, v, preferred_element_type=jnp.float32)
            acc = part if acc is None else acc + part
        total = acc[:, 128:]
        emit(r, acc[:, :128] / total, top * SCALE2 + jnp.log2(total))


def needs(lens_ref, base, rows, ahead, back):
    q_first = base + ahead * rows
    start = jnp.int32(0)
    end = jnp.int32(0)
    for doc in range(lens_ref.shape[0] - 1):
        end = end + lens_ref[doc]
        start = jnp.where(q_first >= end, end, start)
    return start < base + (1 - back) * rows


def fill_bias(lens_ref, base, rows, ref, ahead, back):
    qpos = base + ahead * rows + lax.broadcasted_iota(jnp.int32, (rows, 1), 0)
    starts = doc_start(qpos, lens_ref)
    kpos = base - back * rows + lax.broadcasted_iota(jnp.int32, (1, rows), 1)
    ref[...] = jnp.where((kpos <= qpos) & (kpos >= starts), 0.0, NEG).astype(jnp.float32)


def near_kernel(rows, lens_ref, q_ref, k_ref, v_ref, k1_ref, v1_ref, k2_ref, v2_ref, all_ref, o_ref,
                b0, b1, b2):
    span = lens_ref[lens_ref.shape[0] - 1]
    base = span * rows
    one = (span >= 1) & needs(lens_ref, base, rows, 0, 1)
    two = (span >= 2) & needs(lens_ref, base, rows, 0, 2)

    @pl.when(pl.program_id(0) == 0)
    def _():
        fill_bias(lens_ref, base, rows, b0, 0, 0)
        pl.when(one)(lambda: fill_bias(lens_ref, base, rows, b1, 0, 1))
        pl.when(two)(lambda: fill_bias(lens_ref, base, rows, b2, 0, 2))

    def emit(r, out, lse):
        o_ref[r : r + 128, :] = out.astype(jnp.bfloat16)

    pl.when(two)(
        lambda: attend(q_ref, (k_ref, k1_ref, k2_ref), (v_ref, v1_ref, v2_ref), (b0, b1, b2), emit)
    )
    pl.when(one & jnp.logical_not(two))(
        lambda: attend(q_ref, (k_ref, k1_ref), (v_ref, v1_ref), (b0, b1), emit)
    )
    pl.when(jnp.logical_not(one))(lambda: attend(q_ref, (k_ref,), (v_ref,), (b0,), emit))


def attn_kernel(rows, lens_ref, q_ref, qa_ref, qb_ref, kp_ref, vp_ref, k_ref, v_ref,
                o_ref, lse_ref, oa_ref, ob_ref, b00, b10, b01, b11, b02):
    span = lens_ref[lens_ref.shape[0] - 1]
    base = span * rows

    def reads(ahead, back):
        return needs(lens_ref, base, rows, ahead, back)

    own_prev = (span == 1) & reads(0, 1)
    a_here = ((span == 1) | (span == 2)) & reads(1, 0)
    a_prev = (span == 1) & reads(1, 1)
    b_here = (span == 1) & reads(2, 0)

    @pl.when(pl.program_id(0) == 0)
    def _():
        lse_ref[...] = jnp.zeros_like(lse_ref)

        def fill(ref, ahead, back):
            fill_bias(lens_ref, base, rows, ref, ahead, back)

        fill(b00, 0, 0)
        pl.when(own_prev)(lambda: fill(b01, 0, 1))
        pl.when(a_here)(lambda: fill(b10, 1, 0))
        pl.when(a_prev)(lambda: fill(b11, 1, 1))
        pl.when(b_here)(lambda: fill(b02, 2, 0))

    step = 128
    head_lane = lax.broadcasted_iota(jnp.int32, (step, 128), 1) == pl.program_id(0)

    def emit_own(r, out, lse):
        o_ref[r : r + step, :] = out.astype(jnp.bfloat16)
        lse_ref[r : r + step, :] = jnp.where(head_lane, lse, lse_ref[r : r + step, :])

    eye = lax.broadcasted_iota(jnp.int32, (128, 128), 0) == lax.broadcasted_iota(
        jnp.int32, (128, 128), 1
    )
    stat_iota = lax.broadcasted_iota(jnp.int32, (STAT_ROWS, 128), 0)

    def emit_to(ref):
        stats = [jnp.zeros((STAT_ROWS, 128), jnp.float32)]

        def emit(r, out, lse):
            ref[r : r + step, :] = out.astype(jnp.bfloat16)
            rest = jnp.sum(jnp.where(eye, lse, 0.0), axis=0, keepdims=True)
            for piece in range(3):
                high = rest.astype(jnp.bfloat16).astype(jnp.float32)
                stats[0] = jnp.where(stat_iota == piece * (rows // step) + r // step, high, stats[0])
                rest = rest - high
            if r + step == rows:
                ref[rows:, :] = stats[0].astype(jnp.bfloat16)

        return emit

    def empty(ref):
        ref[:rows, :] = jnp.zeros((rows, 128), jnp.bfloat16)
        ref[rows:, :] = jnp.where(stat_iota < rows // step, NEG, 0.0).astype(jnp.bfloat16)

    pl.when(own_prev)(lambda: attend(q_ref, (kp_ref, k_ref), (vp_ref, v_ref), (b01, b00), emit_own))
    pl.when(jnp.logical_not(own_prev))(lambda: attend(q_ref, (k_ref,), (v_ref,), (b00,), emit_own))
    pl.when(a_prev)(
        lambda: attend(qa_ref, (kp_ref, k_ref), (vp_ref, v_ref), (b11, b10), emit_to(oa_ref))
    )
    pl.when(a_here & jnp.logical_not(a_prev))(
        lambda: attend(qa_ref, (k_ref,), (v_ref,), (b10,), emit_to(oa_ref))
    )
    pl.when(jnp.logical_not(a_here))(lambda: empty(oa_ref))
    pl.when(b_here)(lambda: attend(qb_ref, (k_ref,), (v_ref,), (b02,), emit_to(ob_ref)))
    pl.when(jnp.logical_not(b_here))(lambda: empty(ob_ref))


def merge_kernel(rows, lens_ref, o_ref, lse_ref, ra_ref, rb_ref, all_ref, out_ref):
    span = lens_ref[lens_ref.shape[0] - 1]
    step = 128
    eye = lax.broadcasted_iota(jnp.int32, (128, 128), 0) == lax.broadcasted_iota(
        jnp.int32, (128, 128), 1
    )

    @pl.when(span < 2)
    def _():
        out_ref[...] = o_ref[...]

    @pl.when(span >= 2)
    def _():
        blocks = rows // step
        head_lane = lax.broadcasted_iota(jnp.int32, (step, 128), 1) == pl.program_id(0)
        stat_a = ra_ref[rows:, :].astype(jnp.float32)
        stat_b = rb_ref[rows:, :].astype(jnp.float32)

        def column(stats, i):
            row = (stats[i : i + 1] + stats[blocks + i : blocks + i + 1]) + stats[
                2 * blocks + i : 2 * blocks + i + 1
            ]
            return jnp.sum(jnp.where(eye, row, 0.0), axis=1, keepdims=True)

        for i in range(blocks):
            r = i * step
            own = jnp.sum(jnp.where(head_lane, lse_ref[r : r + step, :], 0.0), axis=1, keepdims=True)
            lse_a = column(stat_a, i)
            lse_b = jnp.where(span == 3, column(stat_b, i), NEG)
            top = jnp.maximum(own, jnp.maximum(lse_a, lse_b))
            w0 = jnp.exp2(own - top)
            w1 = jnp.exp2(lse_a - top)
            w2 = jnp.exp2(lse_b - top)
            total = (
                o_ref[r : r + step, :].astype(jnp.float32) * w0
                + ra_ref[r : r + step, :].astype(jnp.float32) * w1
                + rb_ref[r : r + step, :].astype(jnp.float32) * w2
            )
            out_ref[r : r + step, :] = (total / (w0 + w1 + w2)).astype(jnp.bfloat16)


def attention_fast(attn_query, attn_key, attn_value, lengths, hyena_out):
    rows, cols = attn_query.shape
    span_index = lax.axis_index("seq")
    scalars = jnp.concatenate((lengths, jnp.reshape(span_index, (1,)).astype(jnp.int32)))
    all_heads = cols // HD
    heads = all_heads * 7 // 16
    near = all_heads - 2 * heads
    width = heads * HD
    smem = pl.BlockSpec(memory_space=pltpu.SMEM)
    block = pl.BlockSpec((rows, HD), lambda h: (0, h))
    tall = pl.BlockSpec((rows + STAT_ROWS, HD), lambda h: (0, h))
    packed = pl.BlockSpec((rows, 128), lambda h: (0, 0))

    def at(offset):
        return pl.BlockSpec((rows, HD), lambda h: (0, offset + h))

    def pair(lo, hi):
        return jnp.concatenate((attn_key[:, lo:hi], attn_value[:, lo:hi]), axis=1)

    sent = []
    for c in range(2):
        qc = attn_query[:, c * width : (c + 1) * width]
        qa = lax.ppermute(qc, "seq", [(2, 1), (3, 2)])
        qb = lax.ppermute(qc, "seq", [(3, 1)])
        kv = pair(c * width, (c + 1) * width)
        sent.append((qa, qb, lax.ppermute(kv, "seq", [(0, 1)])))
    kv = pair(2 * width, cols)
    kv1 = lax.ppermute(kv, "seq", [(0, 1), (1, 2), (2, 3)])
    kv2 = lax.ppermute(kv, "seq", [(0, 2), (1, 3)])
    scalars, hyena_out = lax.optimization_barrier((scalars, hyena_out))
    outs = []
    for c in range(2):
        qa, qb, kvp = sent[c]
        whole = at(c * heads)
        own, lse, oa, ob = pl.pallas_call(
            lambda *refs: attn_kernel(rows, *refs),
            grid=(heads,),
            out_shape=(
                jax.ShapeDtypeStruct((rows, width), jnp.bfloat16),
                jax.ShapeDtypeStruct((rows, 128), jnp.float32),
                jax.ShapeDtypeStruct((rows + STAT_ROWS, width), jnp.bfloat16),
                jax.ShapeDtypeStruct((rows + STAT_ROWS, width), jnp.bfloat16),
            ),
            in_specs=[smem, whole, block, block, block, at(heads), whole, whole],
            out_specs=(block, packed, tall, tall),
            scratch_shapes=[pltpu.VMEM((rows, rows), jnp.float32)] * 5,
            compiler_params=pltpu.CompilerParams(vmem_limit_bytes=32 * 2**20),
            cost_estimate=pl.CostEstimate(
                flops=heads * 5 * rows * rows * HD * 4 * 2,
                bytes_accessed=8 * 2**20,
                transcendentals=heads * 5 * rows * rows,
            ),
            name="attend",
        )(scalars, attn_query, qa, qb, kvp, kvp, attn_key, attn_value)
        ra = lax.ppermute(oa, "seq", [(1, 2), (2, 3)])
        rb = lax.ppermute(ob, "seq", [(1, 3)])
        outs.append((own, lse, ra, rb))
        scalars, _ = lax.optimization_barrier((scalars, own))
    anywhere = pl.BlockSpec(memory_space=pl.ANY)
    whole_out = jax.ShapeDtypeStruct((rows, cols), jnp.bfloat16)
    mine = at(2 * heads)
    result = pl.pallas_call(
        lambda *refs: near_kernel(rows, *refs[:8], None, *refs[8:]),
        grid=(near,),
        out_shape=whole_out,
        in_specs=[smem, mine, mine, mine, block, at(near), block, at(near)],
        out_specs=mine,
        scratch_shapes=[pltpu.VMEM((rows, rows), jnp.float32)] * 3,
        compiler_params=pltpu.CompilerParams(vmem_limit_bytes=32 * 2**20),
        cost_estimate=pl.CostEstimate(
            flops=near * 3 * rows * rows * HD * 4 * 2,
            bytes_accessed=4 * 2**20,
            transcendentals=near * 3 * rows * rows,
        ),
        name="near",
    )(scalars, attn_query, attn_key, attn_value, kv1, kv1, kv2, kv2)
    for c in range(2):
        own, lse, ra, rb = outs[c]
        result = pl.pallas_call(
            lambda *refs: merge_kernel(rows, *refs),
            grid=(heads,),
            out_shape=whole_out,
            in_specs=[smem, block, packed, tall, tall, anywhere],
            out_specs=at(c * heads),
            input_output_aliases={5: 0},
            cost_estimate=pl.CostEstimate(
                flops=rows * width * 16, bytes_accessed=4 * 2**20, transcendentals=0
            ),
            name="merge",
        )(scalars, own, lse, ra, rb, result)
    return hyena_out, result


def local(
    features, short_filter, medium_filter, skip_gain, attn_query, attn_key, attn_value, lengths
):
    rows, cols = attn_query.shape
    spans = lax.axis_size("seq")
    taps = medium_filter.shape[0]
    if cols % 128 == 0 and taps % 128 == 0 and rows % taps == 0:
        hyena = hyena_fast
    else:
        hyena = hyena_mix
    hyena_out = hyena(features, short_filter, medium_filter, skip_gain, lengths)
    if spans == 4 and rows % 128 == 0 and rows <= 640 and cols % (16 * HD) == 0:
        return attention_fast(attn_query, attn_key, attn_value, lengths, hyena_out)
    return (hyena_out, attention_mix(attn_query, attn_key, attn_value, lengths))


def solution(mesh):
    in_specs = (
        P(("groups", "seq"), None, ("tensor", "sub")),
        P(None, ("tensor", "sub")),
        P(None, ("tensor", "sub")),
        P(("tensor", "sub")),
        P(("groups", "seq"), ("tensor", "sub")),
        P(("groups", "seq"), ("tensor", "sub")),
        P(("groups", "seq"), ("tensor", "sub")),
        P("groups"),
    )
    out_specs = (P(("groups", "seq"), ("tensor", "sub")), P(("groups", "seq"), ("tensor", "sub")))
    return jax.shard_map(local, mesh=mesh, in_specs=in_specs, out_specs=out_specs, check_vma=False)
```
